256 devices in a mesh: dev: 128 (over z, y, x_hi, core), rhs: 2 (over x_lo).
Axes of the slice: x: 4 (x_hi: 2, x_lo: 2; x = x_hi * 2 + x_lo), y: 4, z: 8, core: 2. Of those that a mesh axis runs over, the one named last changes fastest.
Arguments:
- top_adj: float32 [16, 256, 128, 256], P('rhs', 'dev'), may hold values from -6 to 6
- level1_adj: float32 [16, 128, 512, 128], P('rhs', 'dev'), may hold values from -6 to 6
- image_offsets: int32 [64, 2], P('rhs'), may hold values from -6 to 6
- image_weights: float32 [64], P('rhs'), may hold values from 0.2 to 1
- incidence: float32 [16, 2], replicated, may hold values from -0.6 to 0.6
- child_list: int32 [128, 4], replicated, may hold values from 0 to 511, as said below
- theta_index_top: int32 [128, 3], replicated, may hold values from 0 to 63
- theta_weight_top: float32 [128, 3], replicated, may hold values from -2.7 to 2.7
- phi_weight_top: float32 [256, 3], replicated, may hold values from -2.7 to 2.7
- theta_index_mid: int32 [64, 3], replicated, may hold values from 0 to 31
- theta_weight_mid: float32 [64, 3], replicated, may hold values from -2.7 to 2.7
- phi_weight_mid: float32 [128, 3], replicated, may hold values from -2.7 to 2.7
Outputs:
- level0_adj: float32 [16, 2048, 4096], P('rhs', 'dev')
The draws below stay inside these ranges and needn't reach their ends.
Inputs may be any that keep to these rules, and one draw needn't show every extreme that they name: `child_list`: row b holds the middle-level boxes 4 b to 4 b + 3, each once.
All inputs are finite; a program needn't handle non-finite values.
Results may differ from the reference program's by a relative error of at most 0.0003.
Values sent between devices are 32-bit elements; how exact they have to be, the bound alone decides.
A program may use at most 128 MiB of HBM per device.

```python
import math
import jax
import jax.numpy as jnp
from jax import lax

EXC = 16
NT2 = 128
IMAGES = 64
NT1 = 64
NT0 = 32
NP2 = 256
NP1 = 128
NP0 = 64
NB2 = 128
NB1 = 512


def stencil_rows(key, row_count, column_count):
    centre = jnp.arange(row_count, dtype=jnp.int32)[:, None] // 2 + jnp.arange(3, dtype=jnp.int32)[None, :] - 1
    jitter = jax.random.randint(key, (row_count, 3), -1, 2, dtype=jnp.int32)
    return jnp.clip(centre + jitter, 0, column_count - 1).astype(jnp.int32)


def draw_child_list(key, part):
    box_keys = jax.random.split(jax.random.fold_in(key, 7), NB2)

    def shuffle(single_key):
        return jax.random.permutation(single_key, jnp.arange(4, dtype=jnp.int32))
    orders = jax.vmap(shuffle)(box_keys)
    return (orders + 4 * jnp.arange(NB2, dtype=jnp.int32)[:, None]).astype(jnp.int32)


def draw_theta_index_top(key, part):
    return stencil_rows(jax.random.fold_in(key, 11), NT2, NT1)


def draw_theta_index_mid(key, part):
    return stencil_rows(jax.random.fold_in(key, 13), NT1, NT0)


def set_ends(array, own_key, smallest, largest):
    spot = [jax.random.randint(jax.random.fold_in(own_key, axis), (), 0, length) for axis, length in enumerate(array.shape)]
    widest = array.shape.index(max(array.shape))
    neighbour = spot[:widest] + [(spot[widest] + 1) % array.shape[widest]] + spot[widest + 1:]
    return array.at[tuple(spot)].set(smallest).at[tuple(neighbour)].set(largest)


def shard_levels(rng, shape, shards, least, largest):
    level, own = 1.0, jax.random.fold_in(rng, 6)
    for dim, parts in shards:
        steps = jnp.exp(jax.random.uniform(jax.random.fold_in(own, dim), (parts,), jnp.float32, least / len(shards), largest / len(shards)))
        level = level * jnp.repeat(steps, shape[dim] // parts).reshape([-1 if axis == dim else 1 for axis in range(len(shape))])
    return level


def scatter_about(key, extent, scale, bound, cuts=(), held_as=jnp.bfloat16):
    entries = scale * jax.random.normal(key, extent, jnp.float32)
    if cuts:
        entries = entries * shard_levels(key, extent, cuts, -0.22, 0.18)
    return jnp.clip(entries, -bound, bound).astype(held_as)


def setup_inputs(seed: int = 0) -> dict:
    key_list = jax.random.split(jax.random.key(seed), 13)
    return {
        "top_adj": scatter_about(key_list[0], (EXC, NP2, NB2, 2 * NT2), 1.0, 6.0, ((0, 2), (1, 128)), jnp.float32),
        "level1_adj": scatter_about(key_list[1], (EXC, NP1, NB1, 2 * NT1), 1.0, 6.0, ((0, 2), (1, 128)), jnp.float32),
        "image_offsets": set_ends(jax.random.randint(key_list[2], (IMAGES, 2), -6, 7), jax.random.fold_in(key_list[2], 1), -6, 6).astype(jnp.int32),
        "image_weights": jnp.clip(jnp.exp(math.log(1.0) - 1.609438 * jax.random.uniform(key_list[3], (IMAGES,), jnp.float32) ** shard_levels(key_list[3], (IMAGES,), ((0, 2),), -0.2, 0.2)), 0.2, 1.0),
        "incidence": jnp.clip(jax.random.uniform(key_list[4], (EXC, 2), jnp.float32, -0.6, 0.6), -0.6, 0.6),
        "child_list": draw_child_list(jax.random.fold_in(key_list[12], 71), 0),
        "theta_index_top": draw_theta_index_top(jax.random.fold_in(key_list[12], 71), 0),
        "theta_weight_top": scatter_about(key_list[7], (NT2, 3), 0.45, 2.7, (), jnp.float32),
        "phi_weight_top": scatter_about(key_list[8], (NP2, 3), 0.45, 2.7, (), jnp.float32),
        "theta_index_mid": draw_theta_index_mid(jax.random.fold_in(key_list[12], 71), 0),
        "theta_weight_mid": scatter_about(key_list[10], (NT1, 3), 0.45, 2.7, (), jnp.float32),
        "phi_weight_mid": scatter_about(key_list[11], (NP1, 3), 0.45, 2.7, (), jnp.float32),
    }


PHASE_TOP = 18.85
PHASE_MID = 9.42
LATTICE = 12.57


def directions(theta_count, phi_ids, phi_count):
    theta = (math.pi / theta_count) * (jnp.arange(theta_count, dtype=jnp.float32) + 0.5)
    azimuth = (2.0 * math.pi / phi_count) * phi_ids.astype(jnp.float32)
    sin_theta = jnp.sin(theta)
    along_x = jnp.cos(azimuth)[:, None] * sin_theta[None, :]
    along_y = jnp.sin(azimuth)[:, None] * sin_theta[None, :]
    along_z = jnp.cos(theta)
    return along_x, along_y, along_z


def theta_matrix(index, weight, columns):
    hits = (index[:, :, None] == jnp.arange(columns, dtype=jnp.int32)[None, None, :]).astype(jnp.float32)
    return jnp.sum(weight[:, :, None] * hits, axis=1)


def phi_matrix(weight, row_ids, coarse_count, column_ids):
    target = (row_ids[:, None] // 2 + jnp.arange(3, dtype=jnp.int32)[None, :] - 1) % coarse_count
    hits = (target[:, :, None] == column_ids[None, None, :]).astype(jnp.float32)
    return jnp.sum(weight[:, :, None] * hits, axis=1)


def octant_phase(factor, octant, along_x, along_y, along_z):
    sign_x = 2.0 * (octant % 2) - 1.0
    sign_y = 2.0 * (octant // 2) - 1.0
    angle = factor * (sign_x * along_x + sign_y * along_y - along_z[None, :])
    return jnp.cos(angle), jnp.sin(angle)


def lattice_sum(offsets, weighted, incident, along_x, along_y):
    phase_arg = LATTICE * (
        offsets[:, 0, None, None, None] * (along_x[None, None] - incident[None, :, 0, None, None])
        + offsets[:, 1, None, None, None] * (along_y[None, None] - incident[None, :, 1, None, None]))
    sum_real = jnp.sum(weighted[:, None, None, None] * jnp.cos(phase_arg), axis=0)
    sum_imag = jnp.sum(weighted[:, None, None, None] * jnp.sin(phase_arg), axis=0)
    return sum_real, sum_imag


def upper_level(top_real, top_imag, along_x, along_y, along_z, theta_map, phi_map, children, top_ids):
    summed = None
    for octant in range(4):
        cosine, sine = octant_phase(PHASE_TOP, octant, along_x, along_y, along_z)
        cosine = cosine[:, None, :]
        sine = sine[:, None, :]
        stacked = jnp.stack([top_real * cosine - top_imag * sine, top_real * sine + top_imag * cosine])
        theta_done = jnp.einsum("...pbt,tu->...pbu", stacked, theta_map, precision=lax.Precision.HIGHEST)
        phi_done = jnp.einsum("...pbu,pq->...qbu", theta_done, phi_map, precision=lax.Precision.HIGHEST)
        select_map = (children[:, octant][:, None] - 4 * top_ids[:, None]
                      == jnp.arange(4, dtype=jnp.int32)[None, :]).astype(jnp.float32)
        placed = phi_done[..., None, :] * select_map[:, :, None]
        summed = placed if summed is None else summed + placed
    merged = summed.reshape(summed.shape[:-3] + (summed.shape[-3] * 4, summed.shape[-1]))
    return jnp.concatenate([merged[0], merged[1]], axis=-1)


def lower_level(middle, along_x, along_y, along_z, theta_map, phi_map):
    half_width = middle.shape[-1] // 2
    mid_real = middle[..., :half_width]
    mid_imag = middle[..., half_width:]
    real_parts = []
    imag_parts = []
    for octant in range(4):
        cosine, sine = octant_phase(PHASE_MID, octant, along_x, along_y, along_z)
        cosine = cosine[:, None, :]
        sine = sine[:, None, :]
        real_parts.append(mid_real * cosine - mid_imag * sine)
        imag_parts.append(mid_real * sine + mid_imag * cosine)
    stacked = jnp.stack([jnp.stack(real_parts, axis=-2), jnp.stack(imag_parts, axis=-2)])
    theta_done = jnp.einsum("...pijt,tu->...piju", stacked, theta_map, precision=lax.Precision.HIGHEST)
    phi_done = jnp.einsum("c...piju,pq->...ijqcu", theta_done, phi_map, precision=lax.Precision.HIGHEST)
    result_shape = phi_done.shape
    return phi_done.reshape(result_shape[:-5] + (result_shape[-5] * 4, result_shape[-3] * result_shape[-2] * result_shape[-1]))


def reference(top_adj, level1_adj, image_offsets, image_weights, incidence, child_list,
              theta_index_top, theta_weight_top, phi_weight_top, theta_index_mid, theta_weight_mid, phi_weight_mid):
    top_phi = jnp.arange(NP2, dtype=jnp.int32)
    top_x, top_y, top_z = directions(NT2, top_phi, NP2)
    mid_phi = jnp.arange(NP1, dtype=jnp.int32)
    mid_x, mid_y, mid_z = directions(NT1, mid_phi, NP1)
    theta_top = theta_matrix(theta_index_top, theta_weight_top, NT1)
    phi_top = phi_matrix(phi_weight_top, top_phi, NP1, mid_phi)
    theta_mid = theta_matrix(theta_index_mid, theta_weight_mid, NT0)
    phi_mid = phi_matrix(phi_weight_mid, mid_phi, NP0, jnp.arange(NP0, dtype=jnp.int32))
    offsets = image_offsets.astype(jnp.float32)
    weighted = image_weights * (float(IMAGES) ** -0.5)
    top_ids = jnp.arange(NB2, dtype=jnp.int32)

    def single(inputs):
        top_pattern, mid_pattern, incident = inputs
        sum_real, sum_imag = lattice_sum(offsets, weighted, incident[None, :], top_x, top_y)
        sum_real = sum_real[0][:, None, :]
        sum_imag = sum_imag[0][:, None, :]
        top_real = top_pattern[..., :NT2]
        top_imag = top_pattern[..., NT2:]
        shifted_real = sum_real * top_real + sum_imag * top_imag
        shifted_imag = sum_real * top_imag - sum_imag * top_real
        above = upper_level(shifted_real, shifted_imag, top_x, top_y, top_z, theta_top, phi_top, child_list, top_ids)
        return lower_level(mid_pattern + above, mid_x, mid_y, mid_z, theta_mid, phi_mid)

    return lax.map(single, (top_adj, level1_adj, incidence))
```

```python
import math

import jax
import jax.numpy as jnp
from jax import lax
from jax.experimental import pallas as pl
from jax.experimental.pallas import tpu as pltpu
from jax.sharding import PartitionSpec as P

PHASE_TOP = 18.85
PHASE_MID = 9.42
LATTICE = 12.57

F32 = jnp.float32
BF16 = jnp.bfloat16

EXC = 8
RN = 16
ZN = 8
PAD = 2
BASES = 4
IMAGES = 64


def iota(shape, dim):
    return lax.broadcasted_iota(jnp.int32, shape, dim)


def column(row):
    n = row.shape[1]
    square = jnp.where(iota((n, n), 0) == iota((n, n), 1), jnp.broadcast_to(row, (n, n)), 0.0)
    return jnp.sum(square, axis=1, keepdims=True)


def split(x):
    high = x.astype(BF16)
    return high, (x - high.astype(F32)).astype(BF16)


def dot3(x, w_high, w_low):
    high, low = split(x)
    out = jnp.dot(high, w_high, preferred_element_type=F32)
    out += jnp.dot(low, w_high, preferred_element_type=F32)
    out += jnp.dot(high, w_low, preferred_element_type=F32)
    return out


def bases(factor, theta, azimuth):
    sin_theta = jnp.sin(theta)
    along_x = factor * (jnp.cos(azimuth) * sin_theta)
    along_y = factor * (jnp.sin(azimuth) * sin_theta)
    cos_x, sin_x = jnp.cos(along_x), jnp.sin(along_x)
    cos_y, sin_y = jnp.cos(along_y), jnp.sin(along_y)
    return cos_x * cos_y, sin_x * sin_y, sin_x * cos_y, cos_x * sin_y


def theta_rows(index_ref, weight_ref, columns):
    samples = index_ref.shape[1]
    rows = iota((columns, samples), 0)
    total = jnp.zeros((columns, samples), F32)
    for s in range(3):
        hit = rows == jnp.broadcast_to(index_ref[s : s + 1, :], (columns, samples))
        total += jnp.where(hit, jnp.broadcast_to(weight_ref[s : s + 1, :], (columns, samples)), 0.0)
    return total


def kernel(
    top_hbm, lvl_hbm, off_ref, wgt_ref, inc_ref, child_ref, tit_ref, twt_ref, pwt_ref,
    tim_ref, twm_ref, pwm_ref,
    out_hbm,
    tin, lin, off_p, wgt_p, lattice,
    s1t, s1l, r1t, r1l, hs, hr, g1, sb, r2, ov,
    btab, wtab, btab2, wtab2, signs,
    wab_h, wab_l, wgd_h, wgd_l, w2t, w2_h, w2_l,
    xs, tq, x2, y2,
    sem_tin, sem_lin, sem_img_s, sem_img_r,
    ss_t, rs_t, ss_l, rs_l, ss_h, rs_h, ss_2, rs_2, sem_out,
):
    dev = lax.axis_index("dev")
    rhs = lax.axis_index("rhs")
    z = dev // RN
    r = dev % RN

    barrier = pltpu.get_barrier_semaphore()

    def greet_plane(o, _):
        pl.semaphore_signal(
            barrier, inc=1, device_id={"dev": z * RN + (r + o) % RN},
            device_id_type=pl.DeviceIdType.MESH,
        )
        return 0

    def greet_column(o, _):
        pl.semaphore_signal(
            barrier, inc=1, device_id={"dev": (z + o) % ZN * RN + r},
            device_id_type=pl.DeviceIdType.MESH,
        )
        return 0

    lax.fori_loop(1, RN, greet_plane, 0)
    lax.fori_loop(1, ZN, greet_column, 0)
    pl.semaphore_signal(
        barrier, inc=1, device_id={"rhs": 1 - rhs}, device_id_type=pl.DeviceIdType.MESH
    )

    def start_inputs(e, _):
        pltpu.make_async_copy(lvl_hbm.at[e], lin.at[e], sem_lin.at[e]).start()
        for p in range(2):
            for c in range(2):
                pltpu.make_async_copy(
                    top_hbm.at[e, p, :, pl.ds(c * 128, 128)], tin.at[e, p, c], sem_tin.at[e]
                ).start()
        return 0

    lax.fori_loop(0, EXC, start_inputs, 0)

    def pack_level(e):
        pltpu.make_async_copy(lin.at[e], lin.at[e], sem_lin.at[e]).wait()

        def body(q, _):
            for j in range(4):
                s1l[e, q, j] = lin[e, pl.ds(4 * q + j, ZN, stride=4 * RN), :]
            return 0

        lax.fori_loop(0, RN, body, 0)

    def pack_top(e):
        pltpu.make_async_copy(tin.at[e], tin.at[e], sem_tin.at[e]).wait()
        mine = rhs * EXC + e
        factors = []
        for p in range(2):
            for c in range(2):
                factors.append(jnp.broadcast_to(lattice[p, c, pl.ds(mine, 1), :], (ZN, 128)))

        def body(q, _):
            for p in range(2):
                s_re, s_im = factors[2 * p], factors[2 * p + 1]
                a_re = tin[e, p, 0, pl.ds(q, ZN, stride=RN), :]
                a_im = tin[e, p, 1, pl.ds(q, ZN, stride=RN), :]
                s1t[e, q, 2 * p] = s_re * a_re + s_im * a_im
                s1t[e, q, 2 * p + 1] = s_re * a_im - s_im * a_re
            return 0

        lax.fori_loop(0, RN, body, 0)

    def send_plane(e, source, target, send_sem, recv_sem, first):
        def body(o, _):
            peer = (r + o) % RN
            pltpu.make_async_remote_copy(
                src_ref=source.at[e, peer], dst_ref=target.at[e, first + r],
                send_sem=send_sem.at[e], recv_sem=recv_sem.at[e],
                device_id={"dev": z * RN + peer}, device_id_type=pl.DeviceIdType.MESH,
            ).start()
            return 0

        lax.fori_loop(1, RN, body, 0)
        pltpu.make_async_copy(source.at[e, r], target.at[e, first + r], recv_sem.at[e]).start()

    def wait_bytes(ref, sem):
        pltpu.make_async_copy(ref, ref, sem).wait()

    pack_level(0)
    pl.semaphore_wait(barrier, RN - 1 + ZN - 1 + 1)
    images = []
    for k, (source, target) in enumerate(((off_ref, off_p), (wgt_ref, wgt_p))):
        images.append(
            pltpu.make_async_remote_copy(
                src_ref=source, dst_ref=target, send_sem=sem_img_s.at[k], recv_sem=sem_img_r.at[k],
                device_id={"rhs": 1 - rhs}, device_id_type=pl.DeviceIdType.MESH,
            )
        )
        images[-1].start()
    send_plane(0, s1l, r1l, ss_l, rs_l, 0)
    pack_level(1)
    send_plane(1, s1l, r1l, ss_l, rs_l, 0)

    theta = (math.pi / 128) * (iota((8, 128), 1).astype(F32) + 0.5)
    own_phi = (2 * math.pi / 256) * (2 * dev + iota((8, 128), 0)).astype(F32)
    own_x = jnp.cos(own_phi) * jnp.sin(theta)
    own_y = jnp.sin(own_phi) * jnp.sin(theta)
    for copy in images:
        copy.wait()
    off_x, off_y, weight = [], [], []
    for offsets, weights in ((off_ref, wgt_ref), (off_p, wgt_p)):
        off_x.append(column(offsets[0:1, :].astype(F32)))
        off_y.append(column(offsets[1:2, :].astype(F32)))
        weight.append(column(weights[...]) * (float(IMAGES) ** -0.5))
    off_x = jnp.concatenate(off_x, axis=0)
    off_y = jnp.concatenate(off_y, axis=0)
    weight = jnp.concatenate(weight, axis=0)
    turn = -LATTICE * (off_x * inc_ref[0:1, :] + off_y * inc_ref[1:2, :])
    coef_re = weight * jnp.cos(turn)
    coef_im = weight * jnp.sin(turn)

    def over_images(a, b):
        return lax.dot_general(
            a, b, (((0,), (0,)), ((), ())), precision=lax.Precision.HIGHEST,
            preferred_element_type=F32,
        )

    for p in range(2):
        angle = LATTICE * (off_x * own_x[p : p + 1, :] + off_y * own_y[p : p + 1, :])
        wave_re, wave_im = jnp.cos(angle), jnp.sin(angle)
        lattice[p, 0] = over_images(coef_re, wave_re) - over_images(coef_im, wave_im)
        lattice[p, 1] = over_images(coef_re, wave_im) + over_images(coef_im, wave_re)

    def send_all(e, _):
        pack_top(e)
        send_plane(e, s1t, r1t, ss_t, rs_t, PAD)

        @pl.when(e < EXC - 2)
        def _():
            pack_level(e + 2)
            send_plane(e + 2, s1l, r1l, ss_l, rs_l, 0)

        return 0

    lax.fori_loop(0, EXC, send_all, 0)

    zeros = jnp.zeros((ZN, 128), F32)

    def clear_top(e, _):
        for k in range(PAD):
            for c in range(4):
                r1t[e, k, c] = zeros
                r1t[e, PAD + RN + k, c] = zeros
        return 0

    lax.fori_loop(0, EXC, clear_top, 0)

    def clear_mid(k, _):
        for slot in range(2):
            for i in range(4):
                g1[slot, k, i] = zeros
                g1[slot, RN + 2 * PAD + k, i] = zeros
        return 0

    lax.fori_loop(0, 2 * PAD, clear_mid, 0)

    def clear_weights(k, _):
        for s in range(3):
            for b in range(BASES):
                wtab[k, s, b] = zeros
                wtab[2 * RN + 2 * PAD + k, s, b] = zeros
                wtab2[k, s, b] = zeros
                wtab2[RN + 2 * PAD + k, s, b] = zeros
        return 0

    lax.fori_loop(0, 2 * PAD, clear_weights, 0)

    theta_b = (math.pi / 128) * (iota((32, 128), 1).astype(F32) + 0.5)
    phi_b = (2 * math.pi / 256) * (32 * z + iota((32, 128), 0)).astype(F32)
    for b, value in enumerate(bases(PHASE_TOP, theta_b, phi_b)):
        btab[b] = value
    mid_t = (iota((16, 128), 1) % 64).astype(F32)
    theta_b = (math.pi / 64) * (mid_t + 0.5)
    phi_b = (2 * math.pi / 128) * (16 * z + iota((16, 128), 0)).astype(F32)
    for b, value in enumerate(bases(PHASE_MID, theta_b, phi_b)):
        btab2[b] = value

    def weigh_top(p, _):
        for b in range(BASES):
            row = jnp.broadcast_to(btab[b, pl.ds(p, 1), :], (ZN, 128))
            for s in range(3):
                wtab[2 * PAD + p, s, b] = row * pwt_ref[s, 32 * z + p]
        return 0

    lax.fori_loop(0, 2 * RN, weigh_top, 0)

    def weigh_mid(p, _):
        for b in range(BASES):
            row = jnp.broadcast_to(btab2[b, pl.ds(p, 1), :], (ZN, 128))
            for s in range(3):
                wtab2[2 * PAD + p, s, b] = row * pwm_ref[s, 16 * z + p]
        return 0

    lax.fori_loop(0, RN, weigh_mid, 0)

    own_box = iota((ZN, 128), 1) == RN * iota((ZN, 128), 0) + r
    own_first = (4 * (RN * iota((ZN, 1), 0) + r)).astype(F32)
    places = []
    for j in range(4):
        row = jnp.broadcast_to(child_ref[j : j + 1, :].astype(F32), (ZN, 128))
        places.append(jnp.sum(jnp.where(own_box, row, 0.0), axis=1, keepdims=True) - own_first)
    for i in range(4):
        sign_x = jnp.zeros((ZN, 1), F32)
        sign_y = jnp.zeros((ZN, 1), F32)
        for j in range(4):
            here = jnp.where(places[j] == float(i), 1.0, 0.0)
            sign_x += (2.0 * (j % 2) - 1.0) * here
            sign_y += (2.0 * (j // 2) - 1.0) * here
        signs[i, 0] = jnp.broadcast_to(sign_x * sign_y, (ZN, 128))
        signs[i, 1] = jnp.broadcast_to(sign_x, (ZN, 128))
        signs[i, 2] = jnp.broadcast_to(sign_y, (ZN, 128))

    theta_t = theta_rows(tit_ref, twt_ref, 64)
    along_z = PHASE_TOP * jnp.cos((math.pi / 128) * (iota((1, 128), 1).astype(F32) + 0.5))
    with_cos = theta_t * jnp.cos(along_z)
    with_sin = theta_t * jnp.sin(along_z)

    def square(upper_left, upper_right, lower_left, lower_right):
        upper = jnp.concatenate([upper_left, upper_right], axis=1)
        lower = jnp.concatenate([lower_left, lower_right], axis=1)
        return jnp.concatenate([upper, lower], axis=0)

    wab_h[...], wab_l[...] = split(square(with_cos, with_sin, -with_sin, with_cos).T)
    wgd_h[...], wgd_l[...] = split(square(with_sin, -with_cos, with_cos, with_sin).T)

    theta_m = theta_rows(tim_ref, twm_ref, 32)
    theta_m = jnp.concatenate([theta_m, theta_m], axis=1)
    lane = iota((1, 128), 1)
    along_z = PHASE_MID * jnp.cos((math.pi / 64) * ((lane % 64).astype(F32) + 0.5))
    cos_z, sin_z = jnp.cos(along_z), jnp.sin(along_z)
    low = lane < 64
    rows = (
        (jnp.where(low, cos_z, sin_z), jnp.where(low, -sin_z, cos_z)),
        (jnp.where(low, sin_z, -cos_z), jnp.where(low, cos_z, sin_z)),
    )
    for j in range(4):
        sign_x = 2.0 * (j % 2) - 1.0
        sign_y = 2.0 * (j // 2) - 1.0
        for c in range(2):
            for b, sign in enumerate((1.0, -sign_x * sign_y, sign_x, sign_y)):
                w2t[pl.ds(64 * j + 32 * c, 32), pl.ds(128 * b, 128)] = theta_m * (
                    sign * rows[b // 2][c]
                )
    w2_h[...], w2_l[...] = split(w2t[...].T)

    def upper(e):
        wait_bytes(r1t.at[e, pl.ds(PAD, RN)], rs_t.at[e])
        wait_bytes(r1l.at[e], rs_l.at[e])

        def stencil(q, _):
            total = [[None, None] for _ in range(BASES)]
            for s in range(3):
                for h in range(2):
                    slot = q - s + PAD
                    data = [r1t[e, slot, 2 * h + c] for c in range(2)]
                    for b in range(BASES):
                        factor = wtab[2 * slot + h, s, b]
                        for c in range(2):
                            term = factor * data[c]
                            total[b][c] = term if total[b][c] is None else total[b][c] + term
            for b in range(BASES):
                for c in range(2):
                    xs[b // 2, pl.ds(144 * (b % 2) + 8 * q, 8), pl.ds(128 * c, 128)] = total[b][c]
            return 0

        lax.fori_loop(0, RN + 2, stencil, 0)
        tq[0] = dot3(xs[0], wab_h[...], wab_l[...])
        tq[1] = dot3(xs[1], wgd_h[...], wgd_l[...])

        def combine(q):
            part = [tq[b // 2, pl.ds(144 * (b % 2) + 8 * q, 8), :] for b in range(BASES)]
            return [
                part[0] - signs[i, 0] * part[1] + signs[i, 1] * part[2] + signs[i, 2] * part[3]
                for i in range(4)
            ]

        def inner(q, _):
            for i, value in enumerate(combine(q + 1)):
                g1[e % 2, 2 * PAD + q, i] = r1l[e, q, i] + value
            return 0

        lax.fori_loop(0, RN, inner, 0)
        for side, q in enumerate((0, RN + 1)):
            for i, value in enumerate(combine(q)):
                hs[e, side, i] = value
        for side, plane in enumerate(((z + ZN - 1) % ZN, (z + 1) % ZN)):
            pltpu.make_async_remote_copy(
                src_ref=hs.at[e, side], dst_ref=hr.at[e, side],
                send_sem=ss_h.at[e], recv_sem=rs_h.at[e],
                device_id={"dev": plane * RN + r}, device_id_type=pl.DeviceIdType.MESH,
            ).start()

    half = iota((ZN, 128), 1) < 64

    def lower(e):
        slot = e % 2
        wait_bytes(hr.at[e], rs_h.at[e])
        for i in range(4):
            g1[slot, 2 * PAD + RN - 1, i] += hr[e, 0, i]
            g1[slot, 2 * PAD, i] += hr[e, 1, i]

        def stencil(q, _):
            for i in range(4):
                total = [None] * BASES
                for s in range(3):
                    for h in range(2):
                        place = 2 * (q - s + PAD) + h
                        data = g1[slot, place, i]
                        for b in range(BASES):
                            term = wtab2[place, s, b] * data
                            total[b] = term if total[b] is None else total[b] + term
                for b in range(BASES):
                    x2[pl.ds(32 * q + 8 * i, 8), pl.ds(128 * b, 128)] = total[b]
            return 0

        lax.fori_loop(0, RN // 2 + 2, stencil, 0)
        y2[...] = dot3(x2[...], w2_h[...], w2_l[...])

        for m in range(5):
            first, second = (2 * m + 1, 2 * m + 2) if m < 4 else (9, 0)

            def place(i, _):
                for k in range(2):
                    a = y2[pl.ds(32 * first + 8 * i, 8), pl.ds(128 * k, 128)]
                    b = y2[pl.ds(32 * second + 8 * i, 8), pl.ds(128 * k, 128)]
                    even = jnp.where(half, a, pltpu.roll(b, 64, 1))
                    odd = jnp.where(half, pltpu.roll(a, 64, 1), b)
                    sb[e, m, pl.ds(4 * i + 2 * k, ZN, stride=16), :] = even
                    sb[e, m, pl.ds(4 * i + 2 * k + 1, ZN, stride=16), :] = odd
                return 0

            lax.fori_loop(0, 4, place, 0)

        def send(o, _):
            peer = (z + o) % ZN
            pltpu.make_async_remote_copy(
                src_ref=sb.at[e, :, pl.ds(16 * peer, 16), :], dst_ref=r2.at[e, z],
                send_sem=ss_2.at[e], recv_sem=rs_2.at[e],
                device_id={"dev": peer * RN + r}, device_id_type=pl.DeviceIdType.MESH,
            ).start()
            return 0

        lax.fori_loop(1, ZN, send, 0)
        pltpu.make_async_copy(
            sb.at[e, :, pl.ds(16 * z, 16), :], r2.at[e, z], rs_2.at[e]
        ).start()

    def levels(e, _):
        @pl.when(e < EXC)
        def _():
            upper(e)

        @pl.when(e > 0)
        def _():
            lower(e - 1)

        return 0

    lax.fori_loop(0, EXC + 1, levels, 0)

    low_half = iota((16, 128), 1) < 64

    def assemble(e, _):
        wait_bytes(r2.at[e], rs_2.at[e])
        for k in range(ZN):
            for m in range(4):
                value = r2[e, k, m]
                if m == 0:
                    value = value + jnp.where(low_half, r2[e, (k + ZN - 1) % ZN, 4], 0.0)
                if m == 3:
                    value = value + jnp.where(low_half, 0.0, r2[e, (k + 1) % ZN, 4])
                ov[e, :, pl.ds(512 * k + 128 * m, 128)] = value
        pltpu.make_async_copy(ov.at[e], out_hbm.at[e], sem_out.at[e]).start()
        return 0

    lax.fori_loop(0, EXC, assemble, 0)

    def drain(e, _):
        wait_bytes(s1l.at[e, pl.ds(0, RN - 1)], ss_l.at[e])
        wait_bytes(s1t.at[e, pl.ds(0, RN - 1)], ss_t.at[e])
        wait_bytes(hs.at[e], ss_h.at[e])
        wait_bytes(r2.at[e, pl.ds(0, ZN - 1)], ss_2.at[e])
        pltpu.make_async_copy(ov.at[e], out_hbm.at[e], sem_out.at[e]).wait()
        return 0

    lax.fori_loop(0, EXC, drain, 0)


def local(
    top_adj,
    level1_adj,
    image_offsets,
    image_weights,
    incidence,
    child_list,
    theta_index_top,
    theta_weight_top,
    phi_weight_top,
    theta_index_mid,
    theta_weight_mid,
    phi_weight_mid,
):
    vmem = pl.BlockSpec(memory_space=pltpu.VMEM)
    smem = pl.BlockSpec(memory_space=pltpu.SMEM)
    anywhere = pl.BlockSpec(memory_space=pl.ANY)
    dma = pltpu.SemaphoreType.DMA
    return pl.pallas_call(
        kernel,
        out_shape=jax.ShapeDtypeStruct((EXC, 16, 4096), F32),
        in_specs=[
            anywhere, anywhere, vmem, vmem, vmem, vmem, vmem, vmem, smem, vmem, vmem, smem,
        ],
        out_specs=anywhere,
        scratch_shapes=[
            pltpu.VMEM((EXC, 2, 2, 128, 128), F32),
            pltpu.VMEM((EXC, 512, 128), F32),
            pltpu.VMEM((2, 32), jnp.int32),
            pltpu.VMEM((1, 32), F32),
            pltpu.VMEM((2, 2, 16, 128), F32),
            pltpu.VMEM((EXC, RN, 4, ZN, 128), F32),
            pltpu.VMEM((EXC, RN, 4, ZN, 128), F32),
            pltpu.VMEM((EXC, RN + 2 * PAD, 4, ZN, 128), F32),
            pltpu.VMEM((EXC, RN, 4, ZN, 128), F32),
            pltpu.VMEM((EXC, 2, 4, ZN, 128), F32),
            pltpu.VMEM((EXC, 2, 4, ZN, 128), F32),
            pltpu.VMEM((2, RN + 4 * PAD, 4, ZN, 128), F32),
            pltpu.VMEM((EXC, 5, 128, 128), F32),
            pltpu.VMEM((EXC, ZN, 5, 16, 128), F32),
            pltpu.VMEM((EXC, 16, 4096), F32),
            pltpu.VMEM((BASES, 32, 128), F32),
            pltpu.VMEM((2 * RN + 4 * PAD, 3, BASES, ZN, 128), F32),
            pltpu.VMEM((BASES, 16, 128), F32),
            pltpu.VMEM((RN + 4 * PAD, 3, BASES, ZN, 128), F32),
            pltpu.VMEM((4, 3, ZN, 128), F32),
            pltpu.VMEM((256, 128), BF16),
            pltpu.VMEM((256, 128), BF16),
            pltpu.VMEM((256, 128), BF16),
            pltpu.VMEM((256, 128), BF16),
            pltpu.VMEM((256, 512), F32),
            pltpu.VMEM((512, 256), BF16),
            pltpu.VMEM((512, 256), BF16),
            pltpu.VMEM((2, 288, 256), F32),
            pltpu.VMEM((2, 288, 128), F32),
            pltpu.VMEM((320, 512), F32),
            pltpu.VMEM((320, 256), F32),
            dma((EXC,)), dma((EXC,)), dma((2,)), dma((2,)),
            dma((EXC,)), dma((EXC,)), dma((EXC,)), dma((EXC,)),
            dma((EXC,)), dma((EXC,)), dma((EXC,)), dma((EXC,)), dma((EXC,)),
        ],
        compiler_params=pltpu.CompilerParams(
            collective_id=0, has_side_effects=True, vmem_limit_bytes=50 * 2**20
        ),
        name="two_stage_adjoint",
    )(
        top_adj,
        level1_adj.reshape(EXC, 512, 128),
        image_offsets.T,
        image_weights.reshape(1, 32),
        incidence.T,
        child_list.T,
        theta_index_top.T,
        theta_weight_top.T,
        phi_weight_top.T,
        theta_index_mid.T,
        theta_weight_mid.T,
        phi_weight_mid.T,
    )


def solution(mesh):
    placed = (
        P("rhs", "dev", None, None),
        P("rhs", "dev", None, None),
        P("rhs", None),
        P("rhs"),
        P(),
        P(),
        P(),
        P(),
        P(),
        P(),
        P(),
        P(),
    )
    return jax.shard_map(
        local, mesh=mesh, in_specs=placed, out_specs=P("rhs", "dev", None), check_vma=False
    )
```

```python
import math

import jax
import jax.numpy as jnp
from jax import lax
from jax.experimental import pallas as pl
from jax.experimental.pallas import tpu as pltpu
from jax.sharding import PartitionSpec as P

PHASE_TOP = 18.85
PHASE_MID = 9.42
LATTICE = 12.57

F32 = jnp.float32
BF16 = jnp.bfloat16

EXC = 8
RN = 16
ZN = 8
PAD = 2
BASES = 4
EXT = RN + 4
IMAGES = 64
AHEAD = 3


def iota(shape, dim):
    return lax.broadcasted_iota(jnp.int32, shape, dim)


def column(row):
    n = row.shape[1]
    square = jnp.where(iota((n, n), 0) == iota((n, n), 1), jnp.broadcast_to(row, (n, n)), 0.0)
    return jnp.sum(square, axis=1, keepdims=True)


def split(x):
    high = x.astype(BF16)
    return high, (x - high.astype(F32)).astype(BF16)


def dot3(x, w_high, w_low):
    high, low = split(x)
    out = jnp.dot(high, w_high, preferred_element_type=F32)
    out += jnp.dot(low, w_high, preferred_element_type=F32)
    out += jnp.dot(high, w_low, preferred_element_type=F32)
    return out


def sincos(x):
    turns = jnp.floor(x * (2.0 / math.pi) + 0.5)
    rest = ((x - turns * 1.5703125) - turns * 4.837512969970703e-4) - turns * 7.549789954891882e-8
    z = rest * rest
    sine = ((-1.9515295891e-4 * z + 8.3321608736e-3) * z - 1.6666654611e-1) * z * rest + rest
    cosine = (
        ((2.443315711809948e-5 * z - 1.388731625493765e-3) * z + 4.166664568298827e-2) * z * z
        - 0.5 * z + 1.0
    )
    quadrant = turns.astype(jnp.int32) & 3
    odd = (quadrant & 1) == 1
    out_sin = jnp.where(odd, cosine, sine)
    out_cos = jnp.where(odd, sine, cosine)
    out_sin = jnp.where(quadrant >= 2, -out_sin, out_sin)
    out_cos = jnp.where(((quadrant + 1) & 2) == 2, -out_cos, out_cos)
    return out_sin, out_cos


def bases(factor, theta, azimuth):
    sin_theta, _ = sincos(theta)
    sin_phi, cos_phi = sincos(azimuth)
    sin_x, cos_x = sincos(factor * (cos_phi * sin_theta))
    sin_y, cos_y = sincos(factor * (sin_phi * sin_theta))
    return cos_x * cos_y, sin_x * sin_y, sin_x * cos_y, cos_x * sin_y


def theta_rows(index_ref, weight_ref, columns):
    samples = index_ref.shape[1]
    rows = iota((columns, samples), 0)
    total = jnp.zeros((columns, samples), F32)
    for s in range(3):
        hit = rows == jnp.broadcast_to(index_ref[s : s + 1, :], (columns, samples))
        total += jnp.where(hit, jnp.broadcast_to(weight_ref[s : s + 1, :], (columns, samples)), 0.0)
    return total


def kernel(
    top_hbm, lvl_hbm, off_hbm, wgt_hbm, inc_hbm, child_hbm, tit_hbm, twt_hbm, pwt_hbm,
    tim_hbm, twm_hbm, pwm_hbm,
    out_hbm,
    off_ref, wgt_ref, inc_ref, child_ref, tit_ref, twt_ref, pwt_ref, tim_ref, twm_ref, pwm_ref,
    tin, lin, off_p, wgt_p, lattice,
    s1t, s1l, r1t, r1l, hr, ge, sb, r2, ov,
    btab, wtab, btab2, wtab2, signs,
    wab_h, wab_l, wgd_h, wgd_l, w2t, w2_h, w2_l,
    xs, tq, x2, y2,
    sem_small, sem_tin, sem_lin, sem_img_s, sem_img_r,
    ss_t, rs_t, ss_l, rs_l, ss_h, rs_h, ss_2, rs_2, sem_out,
):
    dev = lax.axis_index("dev")
    rhs = lax.axis_index("rhs")
    z = dev // RN
    r = dev % RN

    barrier = pltpu.get_barrier_semaphore()

    def greet_plane(o, _):
        pl.semaphore_signal(
            barrier, inc=1, device_id={"dev": z * RN + (r + o) % RN},
            device_id_type=pl.DeviceIdType.MESH,
        )
        return 0

    def greet_column(o, _):
        pl.semaphore_signal(
            barrier, inc=1, device_id={"dev": (z + o) % ZN * RN + r},
            device_id_type=pl.DeviceIdType.MESH,
        )
        return 0

    lax.fori_loop(1, RN, greet_plane, 0)
    lax.fori_loop(1, ZN, greet_column, 0)
    pl.semaphore_signal(
        barrier, inc=1, device_id={"rhs": 1 - rhs}, device_id_type=pl.DeviceIdType.MESH
    )

    smalls = [
        pltpu.make_async_copy(source, target, sem_small.at[k])
        for k, (source, target) in enumerate((
            (off_hbm, off_ref), (wgt_hbm, wgt_ref), (inc_hbm, inc_ref), (child_hbm, child_ref),
            (tit_hbm, tit_ref), (twt_hbm, twt_ref), (pwt_hbm, pwt_ref), (tim_hbm, tim_ref),
            (twm_hbm, twm_ref), (pwm_hbm, pwm_ref),
        ))
    ]
    for copy in smalls[:3]:
        copy.start()

    def start_inputs(e, _):
        pltpu.make_async_copy(lvl_hbm.at[e], lin.at[e], sem_lin.at[e]).start()
        for p in range(2):
            for c in range(2):
                pltpu.make_async_copy(
                    top_hbm.at[e, p, :, pl.ds(c * 128, 128)], tin.at[e, p, c], sem_tin.at[e]
                ).start()
        return 0

    lax.fori_loop(0, EXC, start_inputs, 0)
    for copy in smalls[3:]:
        copy.start()

    def pack_level(e):
        pltpu.make_async_copy(lin.at[e], lin.at[e], sem_lin.at[e]).wait()

        def body(q, _):
            for j in range(4):
                s1l[e, q, j] = lin[e, pl.ds(4 * q + j, ZN, stride=4 * RN), :]
            return 0

        lax.fori_loop(0, RN, body, 0)

    def pack_top(e):
        pltpu.make_async_copy(tin.at[e], tin.at[e], sem_tin.at[e]).wait()
        mine = rhs * EXC + e
        factors = []
        for p in range(2):
            for c in range(2):
                factors.append(jnp.broadcast_to(lattice[p, c, pl.ds(mine, 1), :], (ZN, 128)))

        def body(q, _):
            for p in range(2):
                s_re, s_im = factors[2 * p], factors[2 * p + 1]
                a_re = tin[e, p, 0, pl.ds(q, ZN, stride=RN), :]
                a_im = tin[e, p, 1, pl.ds(q, ZN, stride=RN), :]
                s1t[e, q, 2 * p] = s_re * a_re + s_im * a_im
                s1t[e, q, 2 * p + 1] = s_re * a_im - s_im * a_re
            return 0

        lax.fori_loop(0, RN, body, 0)

    def send_plane(e, source, target, send_sem, recv_sem, first):
        def body(o, _):
            peer = (r + o) % RN
            pltpu.make_async_remote_copy(
                src_ref=source.at[e, peer], dst_ref=target.at[e, first + r],
                send_sem=send_sem.at[e], recv_sem=recv_sem.at[e],
                device_id={"dev": z * RN + peer}, device_id_type=pl.DeviceIdType.MESH,
            ).start()
            return 0

        lax.fori_loop(1, RN, body, 0)
        pltpu.make_async_copy(source.at[e, r], target.at[e, first + r], recv_sem.at[e]).start()

    def wait_bytes(ref, sem):
        pltpu.make_async_copy(ref, ref, sem).wait()

    pack_level(0)
    for copy in smalls[:3]:
        copy.wait()
    pl.semaphore_wait(barrier, RN - 1 + ZN - 1 + 1)
    images = []
    for k, (source, target) in enumerate(((off_ref, off_p), (wgt_ref, wgt_p))):
        images.append(
            pltpu.make_async_remote_copy(
                src_ref=source, dst_ref=target, send_sem=sem_img_s.at[k], recv_sem=sem_img_r.at[k],
                device_id={"rhs": 1 - rhs}, device_id_type=pl.DeviceIdType.MESH,
            )
        )
        images[-1].start()
    send_plane(0, s1l, r1l, ss_l, rs_l, 0)

    theta = (math.pi / 128) * (iota((8, 128), 1).astype(F32) + 0.5)
    own_phi = (2 * math.pi / 256) * (2 * dev + iota((8, 128), 0)).astype(F32)
    sin_theta, _ = sincos(theta)
    sin_phi, cos_phi = sincos(own_phi)
    own_x = cos_phi * sin_theta
    own_y = sin_phi * sin_theta
    for copy in images:
        copy.wait()
    off_x, off_y, weight = [], [], []
    for offsets, weights in ((off_ref, wgt_ref), (off_p, wgt_p)):
        off_x.append(column(offsets[0:1, :].astype(F32)))
        off_y.append(column(offsets[1:2, :].astype(F32)))
        weight.append(column(weights[...]) * (float(IMAGES) ** -0.5))
    off_x = jnp.concatenate(off_x, axis=0)
    off_y = jnp.concatenate(off_y, axis=0)
    weight = jnp.concatenate(weight, axis=0)
    turn = -LATTICE * (off_x * inc_ref[0:1, :] + off_y * inc_ref[1:2, :])
    coef_im, coef_re = (weight * value for value in sincos(turn))

    def over_images(a, b):
        return lax.dot_general(
            a, b, (((0,), (0,)), ((), ())), precision=lax.Precision.HIGHEST,
            preferred_element_type=F32,
        )

    for p in range(2):
        angle = LATTICE * (off_x * own_x[p : p + 1, :] + off_y * own_y[p : p + 1, :])
        wave_im, wave_re = sincos(angle)
        lattice[p, 0] = over_images(coef_re, wave_re) - over_images(coef_im, wave_im)
        lattice[p, 1] = over_images(coef_re, wave_im) + over_images(coef_im, wave_re)

    pack_top(0)
    send_plane(0, s1t, r1t, ss_t, rs_t, PAD)

    def send_both(e, _):
        pack_level(e)
        send_plane(e, s1l, r1l, ss_l, rs_l, 0)
        pack_top(e)
        send_plane(e, s1t, r1t, ss_t, rs_t, PAD)
        return 0

    lax.fori_loop(1, AHEAD, send_both, 0)

    zeros = jnp.zeros((ZN, 128), F32)

    def clear_top(e, _):
        for k in range(PAD):
            for c in range(4):
                r1t[e, k, c] = zeros
                r1t[e, PAD + RN + k, c] = zeros
        return 0

    lax.fori_loop(0, EXC, clear_top, 0)

    def clear_weights(k, _):
        for s in range(3):
            for b in range(BASES):
                wtab[k, s, b] = zeros
                wtab[2 * RN + 2 * PAD + k, s, b] = zeros
        return 0

    lax.fori_loop(0, 2 * PAD, clear_weights, 0)

    for copy in smalls[3:]:
        copy.wait()
    theta_b = (math.pi / 128) * (iota((32, 128), 1).astype(F32) + 0.5)
    phi_b = (2 * math.pi / 256) * (32 * z + iota((32, 128), 0)).astype(F32)
    for b, value in enumerate(bases(PHASE_TOP, theta_b, phi_b)):
        btab[b] = value
    mid_t = (iota((24, 128), 1) % 64).astype(F32)
    theta_b = (math.pi / 64) * (mid_t + 0.5)
    phi_b = (2 * math.pi / 128) * (16 * z - 2 + iota((24, 128), 0)).astype(F32)
    for b, value in enumerate(bases(PHASE_MID, theta_b, phi_b)):
        btab2[b] = value

    def weigh_top(p, _):
        for b in range(BASES):
            row = jnp.broadcast_to(btab[b, pl.ds(p, 1), :], (ZN, 128))
            for s in range(3):
                wtab[2 * PAD + p, s, b] = row * pwt_ref[s, 32 * z + p]
        return 0

    lax.fori_loop(0, 2 * RN, weigh_top, 0)

    def weigh_mid(p, _):
        for b in range(BASES):
            row = jnp.broadcast_to(btab2[b, pl.ds(p, 1), :], (ZN, 128))
            for s in range(3):
                wtab2[p, s, b] = row * pwm_ref[s, (16 * z - 2 + p + 128) % 128]
        return 0

    lax.fori_loop(0, EXT, weigh_mid, 0)

    own_box = iota((ZN, 128), 1) == RN * iota((ZN, 128), 0) + r
    own_first = (4 * (RN * iota((ZN, 1), 0) + r)).astype(F32)
    places = []
    for j in range(4):
        row = jnp.broadcast_to(child_ref[j : j + 1, :].astype(F32), (ZN, 128))
        places.append(jnp.sum(jnp.where(own_box, row, 0.0), axis=1, keepdims=True) - own_first)
    for i in range(4):
        sign_x = jnp.zeros((ZN, 1), F32)
        sign_y = jnp.zeros((ZN, 1), F32)
        for j in range(4):
            here = jnp.where(places[j] == float(i), 1.0, 0.0)
            sign_x += (2.0 * (j % 2) - 1.0) * here
            sign_y += (2.0 * (j // 2) - 1.0) * here
        signs[i, 0] = jnp.broadcast_to(sign_x * sign_y, (ZN, 128))
        signs[i, 1] = jnp.broadcast_to(sign_x, (ZN, 128))
        signs[i, 2] = jnp.broadcast_to(sign_y, (ZN, 128))

    theta_t = theta_rows(tit_ref, twt_ref, 64)
    along_z = PHASE_TOP * sincos((math.pi / 128) * (iota((1, 128), 1).astype(F32) + 0.5))[1]
    sin_z, cos_z = sincos(along_z)
    with_cos = theta_t * cos_z
    with_sin = theta_t * sin_z

    def square(upper_left, upper_right, lower_left, lower_right):
        upper = jnp.concatenate([upper_left, upper_right], axis=1)
        lower = jnp.concatenate([lower_left, lower_right], axis=1)
        return jnp.concatenate([upper, lower], axis=0)

    wab_h[...], wab_l[...] = split(square(with_cos, with_sin, -with_sin, with_cos).T)
    wgd_h[...], wgd_l[...] = split(square(with_sin, -with_cos, with_cos, with_sin).T)

    theta_m = theta_rows(tim_ref, twm_ref, 32)
    theta_m = jnp.concatenate([theta_m, theta_m], axis=1)
    lane = iota((1, 128), 1)
    along_z = PHASE_MID * sincos((math.pi / 64) * ((lane % 64).astype(F32) + 0.5))[1]
    sin_z, cos_z = sincos(along_z)
    low = lane < 64
    rows = (
        (jnp.where(low, cos_z, sin_z), jnp.where(low, -sin_z, cos_z)),
        (jnp.where(low, sin_z, -cos_z), jnp.where(low, cos_z, sin_z)),
    )
    for j in range(4):
        sign_x = 2.0 * (j % 2) - 1.0
        sign_y = 2.0 * (j // 2) - 1.0
        for c in range(2):
            for b, sign in enumerate((1.0, -sign_x * sign_y, sign_x, sign_y)):
                w2t[pl.ds(64 * j + 32 * c, 32), pl.ds(128 * b, 128)] = theta_m * (
                    sign * rows[b // 2][c]
                )
    w2_h[...], w2_l[...] = split(w2t[...].T)

    def upper(e):
        wait_bytes(r1t.at[e, pl.ds(PAD, RN)], rs_t.at[e])
        wait_bytes(r1l.at[e], rs_l.at[e])

        def stencil(q, _):
            total = [[None, None] for _ in range(BASES)]
            for s in range(3):
                for h in range(2):
                    slot = q - s + PAD
                    data = [r1t[e, slot, 2 * h + c] for c in range(2)]
                    for b in range(BASES):
                        factor = wtab[2 * slot + h, s, b]
                        for c in range(2):
                            term = factor * data[c]
                            total[b][c] = term if total[b][c] is None else total[b][c] + term
            for b in range(BASES):
                for c in range(2):
                    xs[b // 2, pl.ds(144 * (b % 2) + 8 * q, 8), pl.ds(128 * c, 128)] = total[b][c]
            return 0

        lax.fori_loop(0, RN + 2, stencil, 0)
        tq[0] = dot3(xs[0], wab_h[...], wab_l[...])
        tq[1] = dot3(xs[1], wgd_h[...], wgd_l[...])

        def combine(q):
            part = [tq[b // 2, pl.ds(144 * (b % 2) + 8 * q, 8), :] for b in range(BASES)]
            return [
                part[0] - signs[i, 0] * part[1] + signs[i, 1] * part[2] + signs[i, 2] * part[3]
                for i in range(4)
            ]

        def inner(q, _):
            for i, value in enumerate(combine(q + 1)):
                ge[e, 2 + q, i] = r1l[e, q, i] + value
            return 0

        lax.fori_loop(0, RN, inner, 0)
        for q in (0, RN + 1):
            for i, value in enumerate(combine(q)):
                ge[e, 1 + q, i] = value
        for side, plane in enumerate(((z + ZN - 1) % ZN, (z + 1) % ZN)):
            pltpu.make_async_remote_copy(
                src_ref=ge.at[e, pl.ds(1 + 15 * side, 3)], dst_ref=hr.at[e, side],
                send_sem=ss_h.at[e], recv_sem=rs_h.at[e],
                device_id={"dev": plane * RN + r}, device_id_type=pl.DeviceIdType.MESH,
            ).start()

    half = iota((ZN, 128), 1) < 64

    def lower(e):
        wait_bytes(ge.at[e, pl.ds(0, 6)], ss_h.at[e])
        wait_bytes(hr.at[e], rs_h.at[e])
        for i in range(4):
            ge[e, 0, i] = hr[e, 1, 0, i]
            ge[e, 1, i] += hr[e, 1, 1, i]
            ge[e, 2, i] += hr[e, 1, 2, i]
            ge[e, RN + 1, i] += hr[e, 0, 0, i]
            ge[e, RN + 2, i] += hr[e, 0, 1, i]
            ge[e, RN + 3, i] = hr[e, 0, 2, i]

        def stencil(q, _):
            for i in range(4):
                total = [None] * BASES
                for s in range(3):
                    for h in range(2):
                        place = 2 * (q - s + 2) + h
                        data = ge[e, place, i]
                        for b in range(BASES):
                            term = wtab2[place, s, b] * data
                            total[b] = term if total[b] is None else total[b] + term
                for b in range(BASES):
                    x2[pl.ds(32 * q + 8 * i, 8), pl.ds(128 * b, 128)] = total[b]
            return 0

        lax.fori_loop(0, RN // 2, stencil, 0)
        y2[...] = dot3(x2[...], w2_h[...], w2_l[...])

        for m in range(4):

            def place(i, _):
                for k in range(2):
                    a = y2[pl.ds(64 * m + 8 * i, 8), pl.ds(128 * k, 128)]
                    b = y2[pl.ds(64 * m + 32 + 8 * i, 8), pl.ds(128 * k, 128)]
                    even = jnp.where(half, a, pltpu.roll(b, 64, 1))
                    odd = jnp.where(half, pltpu.roll(a, 64, 1), b)
                    row = 32 * (i // 2) + 8 * m + 4 * (i % 2) + 2 * k
                    sb[e, pl.ds(row, ZN, stride=64), :] = even
                    sb[e, pl.ds(row + 1, ZN, stride=64), :] = odd
                return 0

            lax.fori_loop(0, 4, place, 0)

        def send(o, _):
            peer = (z + o) % ZN
            pltpu.make_async_remote_copy(
                src_ref=sb.at[e, pl.ds(64 * peer, 64), :], dst_ref=r2.at[e, z],
                send_sem=ss_2.at[e], recv_sem=rs_2.at[e],
                device_id={"dev": peer * RN + r}, device_id_type=pl.DeviceIdType.MESH,
            ).start()
            return 0

        lax.fori_loop(1, ZN, send, 0)
        pltpu.make_async_copy(
            sb.at[e, pl.ds(64 * z, 64), :], r2.at[e, z], rs_2.at[e]
        ).start()

    def levels(e, _):
        @pl.when(e < EXC - AHEAD)
        def _():
            send_both(e + AHEAD, 0)

        @pl.when(e < EXC)
        def _():
            upper(e)

        @pl.when(e > 0)
        def _():
            lower(e - 1)

        return 0

    lax.fori_loop(0, EXC + 1, levels, 0)

    def assemble(e, _):
        wait_bytes(r2.at[e], rs_2.at[e])
        for k in range(ZN):
            for i in range(2):
                for m in range(4):
                    ov[e, pl.ds(8 * i, 8), pl.ds(512 * k + 128 * m, 128)] = r2[
                        e, k, pl.ds(32 * i + 8 * m, 8), :
                    ]
        pltpu.make_async_copy(ov.at[e], out_hbm.at[e], sem_out.at[e]).start()
        return 0

    lax.fori_loop(0, EXC, assemble, 0)

    def drain(e, _):
        wait_bytes(s1l.at[e, pl.ds(0, RN - 1)], ss_l.at[e])
        wait_bytes(s1t.at[e, pl.ds(0, RN - 1)], ss_t.at[e])
        wait_bytes(sb.at[e, pl.ds(0, 64 * (ZN - 1))], ss_2.at[e])
        pltpu.make_async_copy(ov.at[e], out_hbm.at[e], sem_out.at[e]).wait()
        return 0

    lax.fori_loop(0, EXC, drain, 0)


def local(
    top_adj,
    level1_adj,
    image_offsets,
    image_weights,
    incidence,
    child_list,
    theta_index_top,
    theta_weight_top,
    phi_weight_top,
    theta_index_mid,
    theta_weight_mid,
    phi_weight_mid,
):
    anywhere = pl.BlockSpec(memory_space=pl.ANY)
    hbm = pl.BlockSpec(memory_space=pltpu.HBM)
    dma = pltpu.SemaphoreType.DMA
    return pl.pallas_call(
        kernel,
        out_shape=jax.ShapeDtypeStruct((EXC, 16, 4096), F32),
        in_specs=[hbm] * 12,
        out_specs=anywhere,
        scratch_shapes=[
            pltpu.VMEM((2, 32), jnp.int32),
            pltpu.VMEM((1, 32), F32),
            pltpu.VMEM((2, 16), F32),
            pltpu.VMEM((4, 128), jnp.int32),
            pltpu.VMEM((3, 128), jnp.int32),
            pltpu.VMEM((3, 128), F32),
            pltpu.SMEM((3, 256), F32),
            pltpu.VMEM((3, 64), jnp.int32),
            pltpu.VMEM((3, 64), F32),
            pltpu.SMEM((3, 128), F32),
            pltpu.VMEM((EXC, 2, 2, 128, 128), F32),
            pltpu.VMEM((EXC, 512, 128), F32),
            pltpu.VMEM((2, 32), jnp.int32),
            pltpu.VMEM((1, 32), F32),
            pltpu.VMEM((2, 2, 16, 128), F32),
            pltpu.VMEM((EXC, RN, 4, ZN, 128), F32),
            pltpu.VMEM((EXC, RN, 4, ZN, 128), F32),
            pltpu.VMEM((EXC, RN + 2 * PAD, 4, ZN, 128), F32),
            pltpu.VMEM((EXC, RN, 4, ZN, 128), F32),
            pltpu.VMEM((EXC, 2, 3, 4, ZN, 128), F32),
            pltpu.VMEM((EXC, EXT, 4, ZN, 128), F32),
            pltpu.VMEM((EXC, 512, 128), F32),
            pltpu.VMEM((EXC, ZN, 64, 128), F32),
            pltpu.VMEM((EXC, 16, 4096), F32),
            pltpu.VMEM((BASES, 32, 128), F32),
            pltpu.VMEM((2 * RN + 4 * PAD, 3, BASES, ZN, 128), F32),
            pltpu.VMEM((BASES, 24, 128), F32),
            pltpu.VMEM((EXT, 3, BASES, ZN, 128), F32),
            pltpu.VMEM((4, 3, ZN, 128), F32),
            pltpu.VMEM((256, 128), BF16),
            pltpu.VMEM((256, 128), BF16),
            pltpu.VMEM((256, 128), BF16),
            pltpu.VMEM((256, 128), BF16),
            pltpu.VMEM((256, 512), F32),
            pltpu.VMEM((512, 256), BF16),
            pltpu.VMEM((512, 256), BF16),
            pltpu.VMEM((2, 288, 256), F32),
            pltpu.VMEM((2, 288, 128), F32),
            pltpu.VMEM((256, 512), F32),
            pltpu.VMEM((256, 256), F32),
            dma((10,)), dma((EXC,)), dma((EXC,)), dma((2,)), dma((2,)),
            dma((EXC,)), dma((EXC,)), dma((EXC,)), dma((EXC,)),
            dma((EXC,)), dma((EXC,)), dma((EXC,)), dma((EXC,)), dma((EXC,)),
        ],
        compiler_params=pltpu.CompilerParams(
            collective_id=0, has_side_effects=True, vmem_limit_bytes=50 * 2**20
        ),
        name="two_stage_adjoint",
    )(*(
        pltpu.with_memory_space_constraint(x, pltpu.HBM)
        for x in (
            top_adj,
            level1_adj.reshape(EXC, 512, 128),
            image_offsets.T,
            image_weights.reshape(1, 32),
            incidence.T,
            child_list.T,
            theta_index_top.T,
            theta_weight_top.T,
            phi_weight_top.T,
            theta_index_mid.T,
            theta_weight_mid.T,
            phi_weight_mid.T,
        )
    ))


def solution(mesh):
    placed = (
        P("rhs", "dev", None, None),
        P("rhs", "dev", None, None),
        P("rhs", None),
        P("rhs"),
        P(),
        P(),
        P(),
        P(),
        P(),
        P(),
        P(),
        P(),
    )
    return jax.shard_map(
        local, mesh=mesh, in_specs=placed, out_specs=P("rhs", "dev", None), check_vma=False
    )
```

```python
import math

import jax
import jax.numpy as jnp
from jax import lax
from jax.experimental import pallas as pl
from jax.experimental.pallas import tpu as pltpu
from jax.sharding import PartitionSpec as P

PHASE_TOP = 18.85
PHASE_MID = 9.42
LATTICE = 12.57

F32 = jnp.float32
BF16 = jnp.bfloat16

EXC = 8
RN = 16
ZN = 8
PAD = 2
BASES = 4
IMAGES = 64
AHEAD = 1
LAG = 2
ROWS = 72


FAR_FIRST = (
    (2, 2), (2, 3), (1, 2), (3, 3), (3, 2), (1, 3), (2, 0), (0, 2), (2, 1), (0, 3),
    (1, 0), (3, 1), (3, 0), (1, 1), (0, 1),
)


def iota(shape, dim):
    return lax.broadcasted_iota(jnp.int32, shape, dim)


def column(row):
    n = row.shape[1]
    square = jnp.where(iota((n, n), 0) == iota((n, n), 1), jnp.broadcast_to(row, (n, n)), 0.0)
    return jnp.sum(square, axis=1, keepdims=True)


def split(x):
    high = x.astype(BF16)
    return high, (x - high.astype(F32)).astype(BF16)


def dot3(x, w_high, w_low):
    high, low = split(x)
    out = jnp.dot(high, w_high, preferred_element_type=F32)
    out += jnp.dot(low, w_high, preferred_element_type=F32)
    out += jnp.dot(high, w_low, preferred_element_type=F32)
    return out


def sincos(x):
    turns = jnp.floor(x * (2.0 / math.pi) + 0.5)
    rest = ((x - turns * 1.5703125) - turns * 4.837512969970703e-4) - turns * 7.549789954891882e-8
    z = rest * rest
    sine = ((-1.9515295891e-4 * z + 8.3321608736e-3) * z - 1.6666654611e-1) * z * rest + rest
    cosine = (
        ((2.443315711809948e-5 * z - 1.388731625493765e-3) * z + 4.166664568298827e-2) * z * z
        - 0.5 * z + 1.0
    )
    quadrant = turns.astype(jnp.int32) & 3
    odd = (quadrant & 1) == 1
    out_sin = jnp.where(odd, cosine, sine)
    out_cos = jnp.where(odd, sine, cosine)
    out_sin = jnp.where(quadrant >= 2, -out_sin, out_sin)
    out_cos = jnp.where(((quadrant + 1) & 2) == 2, -out_cos, out_cos)
    return out_sin, out_cos


def bases(factor, theta, azimuth):
    sin_theta, _ = sincos(theta)
    sin_phi, cos_phi = sincos(azimuth)
    sin_x, cos_x = sincos(factor * (cos_phi * sin_theta))
    sin_y, cos_y = sincos(factor * (sin_phi * sin_theta))
    return cos_x * cos_y, sin_x * sin_y, sin_x * cos_y, cos_x * sin_y


def theta_rows(index_ref, weight_ref, columns):
    samples = index_ref.shape[1]
    rows = iota((columns, samples), 0)
    total = jnp.zeros((columns, samples), F32)
    for s in range(3):
        hit = rows == jnp.broadcast_to(index_ref[s : s + 1, :], (columns, samples))
        total += jnp.where(hit, jnp.broadcast_to(weight_ref[s : s + 1, :], (columns, samples)), 0.0)
    return total


def kernel(
    top_hbm, lvl_hbm, off_hbm, wgt_hbm, inc_hbm, child_hbm, tit_hbm, twt_hbm, pwt_hbm,
    tim_hbm, twm_hbm, pwm_hbm,
    out_hbm,
    off_ref, wgt_ref, inc_ref, child_ref, tit_ref, twt_ref, pwt_ref, tim_ref, twm_ref, pwm_ref,
    tin, lin, lat_own, lat_far, lattice,
    s1t, s1l, r1t, r1l, sb, r2, gq, ot, ov,
    btab, wtab, wb, wtab2, signs,
    wab_h, wab_l, wgd_h, wgd_l, w2t, w2_h, w2_l,
    xs, tq, x2, y2,
    sem_small, sem_tin, sem_lin, sem_img_s, sem_img_r,
    ss_t, rs_t, ss_l, rs_l, ss_2, rs_2, sem_out,
):
    dev = lax.axis_index("dev")
    rhs = lax.axis_index("rhs")
    z = dev // RN
    r = dev % RN

    barrier = pltpu.get_barrier_semaphore()

    def greet_plane(o, _):
        pl.semaphore_signal(
            barrier, inc=1, device_id={"dev": z * RN + (r + o) % RN},
            device_id_type=pl.DeviceIdType.MESH,
        )
        return 0

    def greet_column(o, _):
        pl.semaphore_signal(
            barrier, inc=1, device_id={"dev": (z + o) % ZN * RN + r},
            device_id_type=pl.DeviceIdType.MESH,
        )
        return 0

    lax.fori_loop(1, RN, greet_plane, 0)
    lax.fori_loop(1, ZN, greet_column, 0)
    pl.semaphore_signal(
        barrier, inc=1, device_id={"rhs": 1 - rhs}, device_id_type=pl.DeviceIdType.MESH
    )

    smalls = [
        pltpu.make_async_copy(source, target, sem_small.at[k])
        for k, (source, target) in enumerate((
            (off_hbm, off_ref), (wgt_hbm, wgt_ref), (inc_hbm, inc_ref), (child_hbm, child_ref),
            (tit_hbm, tit_ref), (twt_hbm, twt_ref), (pwt_hbm, pwt_ref), (tim_hbm, tim_ref),
            (twm_hbm, twm_ref), (pwm_hbm, pwm_ref),
        ))
    ]
    for copy in smalls[:3]:
        copy.start()

    def start_inputs(e, _):
        pltpu.make_async_copy(lvl_hbm.at[e], lin.at[e], sem_lin.at[e]).start()
        for p in range(2):
            for c in range(2):
                pltpu.make_async_copy(
                    top_hbm.at[e, p, :, pl.ds(c * 128, 128)], tin.at[e, p, c], sem_tin.at[e]
                ).start()
        return 0

    lax.fori_loop(0, EXC, start_inputs, 0)
    for copy in smalls[3:]:
        copy.start()

    def pack_level(e):
        pltpu.make_async_copy(lin.at[e], lin.at[e], sem_lin.at[e]).wait()

        def body(q, _):
            for j in range(4):
                s1l[e, q, j] = lin[e, pl.ds(4 * q + j, ZN, stride=4 * RN), :]
            return 0

        lax.fori_loop(0, RN, body, 0)

    def pack_top(e):
        pltpu.make_async_copy(tin.at[e], tin.at[e], sem_tin.at[e]).wait()
        factors = []
        for p in range(2):
            for c in range(2):
                factors.append(jnp.broadcast_to(lattice[p, c, pl.ds(e, 1), :], (ZN, 128)))

        def body(q, _):
            for p in range(2):
                s_re, s_im = factors[2 * p], factors[2 * p + 1]
                a_re = tin[e, p, 0, pl.ds(q, ZN, stride=RN), :]
                a_im = tin[e, p, 1, pl.ds(q, ZN, stride=RN), :]
                s1t[e, q, 2 * p] = s_re * a_re + s_im * a_im
                s1t[e, q, 2 * p + 1] = s_re * a_im - s_im * a_re
            return 0

        lax.fori_loop(0, RN, body, 0)

    def send_plane(e, source, target, send_sem, recv_sem, first):
        for over, across in FAR_FIRST:
            peer = (
                (r // 4 + over) % 4 * 4 + (r // 2 + across // 2) % 2 * 2 + (r + across) % 2
            )
            pltpu.make_async_remote_copy(
                src_ref=source.at[e, peer], dst_ref=target.at[e, first + r],
                send_sem=send_sem.at[e], recv_sem=recv_sem.at[e],
                device_id={"dev": z * RN + peer}, device_id_type=pl.DeviceIdType.MESH,
            ).start()
        pltpu.make_async_copy(source.at[e, r], target.at[e, first + r], recv_sem.at[e]).start()

    def wait_bytes(ref, sem):
        pltpu.make_async_copy(ref, ref, sem).wait()

    for copy in smalls[:3]:
        copy.wait()
    theta = (math.pi / 128) * (iota((8, 128), 1).astype(F32) + 0.5)
    own_phi = (2 * math.pi / 256) * (2 * dev + iota((8, 128), 0)).astype(F32)
    sin_theta, _ = sincos(theta)
    sin_phi, cos_phi = sincos(own_phi)
    own_x = cos_phi * sin_theta
    own_y = sin_phi * sin_theta
    off_x = column(off_ref[0:1, :].astype(F32))
    off_y = column(off_ref[1:2, :].astype(F32))
    weight = column(wgt_ref[...]) * (float(IMAGES) ** -0.5)
    turn = -LATTICE * (off_x * inc_ref[0:1, :] + off_y * inc_ref[1:2, :])
    coef_im, coef_re = (weight * value for value in sincos(turn))
    waves = []
    for p in range(2):
        angle = LATTICE * (off_x * own_x[p : p + 1, :] + off_y * own_y[p : p + 1, :])
        waves.extend(reversed(sincos(angle)))
    waves = jnp.concatenate(waves, axis=1)
    with_re, with_im = (
        lax.dot_general(
            coef, waves, (((0,), (0,)), ((), ())), precision=lax.Precision.HIGHEST,
            preferred_element_type=F32,
        )
        for coef in (coef_re, coef_im)
    )
    for p in range(2):
        at = 256 * p
        total = (
            with_re[:, at : at + 128] - with_im[:, at + 128 : at + 256],
            with_re[:, at + 128 : at + 256] + with_im[:, at : at + 128],
        )
        for c in range(2):
            for k in range(2):
                lat_own[k, p, c] = total[c][EXC * k : EXC * (k + 1), :]

    pack_level(0)
    pl.semaphore_wait(barrier, RN - 1 + ZN - 1 + 1)
    swap = pltpu.make_async_remote_copy(
        src_ref=lat_own.at[1 - rhs], dst_ref=lat_far, send_sem=sem_img_s, recv_sem=sem_img_r,
        device_id={"rhs": 1 - rhs}, device_id_type=pl.DeviceIdType.MESH,
    )
    swap.start()
    send_plane(0, s1l, r1l, ss_l, rs_l, 0)
    swap.wait()
    lattice[...] = lat_own[rhs] + lat_far[...]
    pack_top(0)
    send_plane(0, s1t, r1t, ss_t, rs_t, PAD)

    def send_both(e, _):
        pack_level(e)
        send_plane(e, s1l, r1l, ss_l, rs_l, 0)
        pack_top(e)
        send_plane(e, s1t, r1t, ss_t, rs_t, PAD)
        return 0

    lax.fori_loop(1, AHEAD, send_both, 0)

    zeros = jnp.zeros((ZN, 128), F32)

    def clear_top(e, _):
        for k in range(PAD):
            for c in range(4):
                r1t[e, k, c] = zeros
                r1t[e, PAD + RN + k, c] = zeros
        return 0

    lax.fori_loop(0, EXC, clear_top, 0)

    def clear_weights(k, _):
        for s in range(3):
            for b in range(BASES):
                wtab[k, s, b] = zeros
                wtab[2 * RN + 2 * PAD + k, s, b] = zeros
        return 0

    lax.fori_loop(0, 2 * PAD, clear_weights, 0)

    for copy in smalls[3:]:
        copy.wait()
    theta_b = (math.pi / 128) * (iota((32, 128), 1).astype(F32) + 0.5)
    phi_b = (2 * math.pi / 256) * (32 * z + iota((32, 128), 0)).astype(F32)
    for b, value in enumerate(bases(PHASE_TOP, theta_b, phi_b)):
        btab[b] = value
    mid_t = (iota((144, 128), 1) % 64).astype(F32)
    theta_b = (math.pi / 64) * (mid_t + 0.5)
    mid_p = (iota((144, 128), 0) + 120) % 128
    mid_bases = bases(PHASE_MID, theta_b, (2 * math.pi / 128) * mid_p.astype(F32))
    own_lane = mid_p == iota((144, 128), 1)
    for s in range(3):
        row = jnp.broadcast_to(pwm_ref[s : s + 1, :], (144, 128))
        weights = jnp.sum(jnp.where(own_lane, row, 0.0), axis=1, keepdims=True)
        for b in range(BASES):
            wb[s, b] = weights * mid_bases[b]

    def weigh_top(p, _):
        for b in range(BASES):
            row = jnp.broadcast_to(btab[b, pl.ds(p, 1), :], (ZN, 128))
            for s in range(3):
                wtab[2 * PAD + p, s, b] = row * pwt_ref[s, 32 * z + p]
        return 0

    lax.fori_loop(0, 2 * RN, weigh_top, 0)

    def weigh_mid(g, _):
        for odd in range(2):
            for s in range(3):
                for h in range(2):
                    first = 32 * g + 2 * (odd - s) + 10 + h
                    for b in range(BASES):
                        wtab2[g, odd, s, h, b] = wb[s, b, pl.ds(first, 8, stride=4), :]
        return 0

    lax.fori_loop(0, 4, weigh_mid, 0)

    own_box = iota((ZN, 128), 1) == RN * iota((ZN, 128), 0) + r
    own_first = (4 * (RN * iota((ZN, 1), 0) + r)).astype(F32)
    places = []
    for j in range(4):
        row = jnp.broadcast_to(child_ref[j : j + 1, :].astype(F32), (ZN, 128))
        places.append(jnp.sum(jnp.where(own_box, row, 0.0), axis=1, keepdims=True) - own_first)
    for i in range(4):
        sign_x = jnp.zeros((ZN, 1), F32)
        sign_y = jnp.zeros((ZN, 1), F32)
        for j in range(4):
            here = jnp.where(places[j] == float(i), 1.0, 0.0)
            sign_x += (2.0 * (j % 2) - 1.0) * here
            sign_y += (2.0 * (j // 2) - 1.0) * here
        signs[i, 0] = jnp.broadcast_to(sign_x * sign_y, (ZN, 128))
        signs[i, 1] = jnp.broadcast_to(sign_x, (ZN, 128))
        signs[i, 2] = jnp.broadcast_to(sign_y, (ZN, 128))

    theta_t = theta_rows(tit_ref, twt_ref, 64)
    along_z = PHASE_TOP * sincos((math.pi / 128) * (iota((1, 128), 1).astype(F32) + 0.5))[1]
    sin_z, cos_z = sincos(along_z)
    with_cos = theta_t * cos_z
    with_sin = theta_t * sin_z

    def square(upper_left, upper_right, lower_left, lower_right):
        upper = jnp.concatenate([upper_left, upper_right], axis=1)
        lower = jnp.concatenate([lower_left, lower_right], axis=1)
        return jnp.concatenate([upper, lower], axis=0)

    wab_h[...], wab_l[...] = split(square(with_cos, with_sin, -with_sin, with_cos).T)
    wgd_h[...], wgd_l[...] = split(square(with_sin, -with_cos, with_cos, with_sin).T)

    theta_m = theta_rows(tim_ref, twm_ref, 32)
    theta_m = jnp.concatenate([theta_m, theta_m], axis=1)
    lane = iota((1, 128), 1)
    along_z = PHASE_MID * sincos((math.pi / 64) * ((lane % 64).astype(F32) + 0.5))[1]
    sin_z, cos_z = sincos(along_z)
    low = lane < 64
    rows = (
        (jnp.where(low, cos_z, sin_z), jnp.where(low, -sin_z, cos_z)),
        (jnp.where(low, sin_z, -cos_z), jnp.where(low, cos_z, sin_z)),
    )
    for j in range(4):
        sign_x = 2.0 * (j % 2) - 1.0
        sign_y = 2.0 * (j // 2) - 1.0
        for c in range(2):
            for b, sign in enumerate((1.0, -sign_x * sign_y, sign_x, sign_y)):
                w2t[pl.ds(64 * j + 32 * c, 32), pl.ds(128 * b, 128)] = theta_m * (
                    sign * rows[b // 2][c]
                )
    w2_h[...], w2_l[...] = split(w2t[...].T)

    def upper(e):
        wait_bytes(r1t.at[e, pl.ds(PAD, RN)], rs_t.at[e])
        wait_bytes(r1l.at[e], rs_l.at[e])

        def stencil(q, _):
            total = [[None, None] for _ in range(BASES)]
            for s in range(3):
                for h in range(2):
                    slot = q - s + PAD
                    data = [r1t[e, slot, 2 * h + c] for c in range(2)]
                    for b in range(BASES):
                        factor = wtab[2 * slot + h, s, b]
                        for c in range(2):
                            term = factor * data[c]
                            total[b][c] = term if total[b][c] is None else total[b][c] + term
            for b in range(BASES):
                for c in range(2):
                    xs[b // 2, pl.ds(144 * (b % 2) + 8 * q, 8), pl.ds(128 * c, 128)] = total[b][c]
            return 0

        lax.fori_loop(0, RN + 2, stencil, 0)
        tq[0] = dot3(xs[0], wab_h[...], wab_l[...])
        tq[1] = dot3(xs[1], wgd_h[...], wgd_l[...])

        def combine(q):
            part = [tq[b // 2, pl.ds(144 * (b % 2) + 8 * q, 8), :] for b in range(BASES)]
            return [
                part[0] - signs[i, 0] * part[1] + signs[i, 1] * part[2] + signs[i, 2] * part[3]
                for i in range(4)
            ]

        def inner(q, _):
            for i, value in enumerate(combine(q + 1)):
                sb[e, pl.ds(16 * i + q, ZN, stride=ROWS), :] = r1l[e, q, i] + value
            return 0

        lax.fori_loop(0, RN, inner, 0)
        for side, q in enumerate((0, RN + 1)):
            for i, value in enumerate(combine(q)):
                sb[e, pl.ds(64 + 2 * i + side, ZN, stride=ROWS), :] = value

        for o in (4, 3, 5, 2, 6, 1, 7):
            peer = (z + o) % ZN
            pltpu.make_async_remote_copy(
                src_ref=sb.at[e, pl.ds(ROWS * peer, ROWS), :],
                dst_ref=r2.at[e, pl.ds(ROWS * z, ROWS), :],
                send_sem=ss_2.at[e], recv_sem=rs_2.at[e],
                device_id={"dev": peer * RN + r}, device_id_type=pl.DeviceIdType.MESH,
            ).start()
        pltpu.make_async_copy(
            sb.at[e, pl.ds(ROWS * z, ROWS), :], r2.at[e, pl.ds(ROWS * z, ROWS), :], rs_2.at[e]
        ).start()

    half = iota((8, 128), 1) < 64

    def lower(e):
        wait_bytes(r2.at[e], rs_2.at[e])

        def gather(k, _):
            for i in range(4):
                gq[i, pl.ds(8 + 16 * k, 16), :] = r2[e, pl.ds(ROWS * k + 16 * i, 16), :]
            return 0

        lax.fori_loop(0, ZN, gather, 0)
        for i in range(4):
            gq[i, pl.ds(0, 8), :] = zeros
            gq[i, pl.ds(136, 8), :] = zeros
            for side in range(2):
                halo = r2[e, pl.ds(64 + 2 * i + side, ZN, stride=ROWS), :]
                gq[i, pl.ds(7 + 17 * side, ZN, stride=16), :] += halo
            gq[i, pl.ds(135, 1), :] += gq[i, pl.ds(7, 1), :]
            gq[i, pl.ds(8, 1), :] += gq[i, pl.ds(136, 1), :]
            gq[i, pl.ds(6, 2), :] = gq[i, pl.ds(134, 2), :]
            gq[i, pl.ds(136, 2), :] = gq[i, pl.ds(8, 2), :]

        def stencil(g, _):
            for i in range(4):
                data = {
                    (shift, h): gq[i, pl.ds(32 * g + 2 * shift + 10 + h, 8, stride=4), :]
                    for shift in range(-2, 2)
                    for h in range(2)
                }
                for odd in range(2):
                    for b in range(BASES):
                        total = None
                        for s in range(3):
                            for h in range(2):
                                term = wtab2[g, odd, s, h, b] * data[odd - s, h]
                                total = term if total is None else total + term
                        x2[pl.ds(128 * odd + 32 * i + 8 * g, 8), pl.ds(128 * b, 128)] = total
            return 0

        lax.fori_loop(0, 4, stencil, 0)
        y2[...] = dot3(x2[...], w2_h[...], w2_l[...])

        def place(g, _):
            for i in range(4):
                for k in range(2):
                    a = y2[pl.ds(32 * i + 8 * g, 8), pl.ds(128 * k, 128)]
                    b = y2[pl.ds(128 + 32 * i + 8 * g, 8), pl.ds(128 * k, 128)]
                    row = 256 * (i // 2) + 64 * g + 4 * (i % 2) + 2 * k
                    ot[pl.ds(row, 8, stride=8), :] = jnp.where(half, a, pltpu.roll(b, 64, 1))
                    ot[pl.ds(row + 1, 8, stride=8), :] = jnp.where(half, pltpu.roll(a, 64, 1), b)
            return 0

        lax.fori_loop(0, 4, place, 0)
        for k in range(2):
            for m in range(32):
                ov[e, pl.ds(8 * k, 8), pl.ds(128 * m, 128)] = ot[pl.ds(256 * k + 8 * m, 8), :]
        pltpu.make_async_copy(ov.at[e], out_hbm.at[e], sem_out.at[e]).start()

    def levels(e, _):
        @pl.when(e < EXC - AHEAD)
        def _():
            send_both(e + AHEAD, 0)

        @pl.when(e < EXC)
        def _():
            upper(e)

        @pl.when(e >= LAG)
        def _():
            lower(e - LAG)

        return 0

    lax.fori_loop(0, EXC + LAG, levels, 0)

    def drain(e, _):
        wait_bytes(s1l.at[e, pl.ds(0, RN - 1)], ss_l.at[e])
        wait_bytes(s1t.at[e, pl.ds(0, RN - 1)], ss_t.at[e])
        wait_bytes(sb.at[e, pl.ds(0, ROWS * (ZN - 1))], ss_2.at[e])
        pltpu.make_async_copy(ov.at[e], out_hbm.at[e], sem_out.at[e]).wait()
        return 0

    lax.fori_loop(0, EXC, drain, 0)


def local(
    top_adj,
    level1_adj,
    image_offsets,
    image_weights,
    incidence,
    child_list,
    theta_index_top,
    theta_weight_top,
    phi_weight_top,
    theta_index_mid,
    theta_weight_mid,
    phi_weight_mid,
):
    anywhere = pl.BlockSpec(memory_space=pl.ANY)
    hbm = pl.BlockSpec(memory_space=pltpu.HBM)
    dma = pltpu.SemaphoreType.DMA
    return pl.pallas_call(
        kernel,
        out_shape=jax.ShapeDtypeStruct((EXC, 16, 4096), F32),
        in_specs=[hbm] * 12,
        out_specs=anywhere,
        scratch_shapes=[
            pltpu.VMEM((2, 32), jnp.int32),
            pltpu.VMEM((1, 32), F32),
            pltpu.VMEM((2, 16), F32),
            pltpu.VMEM((4, 128), jnp.int32),
            pltpu.VMEM((3, 128), jnp.int32),
            pltpu.VMEM((3, 128), F32),
            pltpu.SMEM((3, 256), F32),
            pltpu.VMEM((3, 64), jnp.int32),
            pltpu.VMEM((3, 64), F32),
            pltpu.VMEM((3, 128), F32),
            pltpu.VMEM((EXC, 2, 2, 128, 128), F32),
            pltpu.VMEM((EXC, 512, 128), F32),
            pltpu.VMEM((2, 2, 2, EXC, 128), F32),
            pltpu.VMEM((2, 2, EXC, 128), F32),
            pltpu.VMEM((2, 2, EXC, 128), F32),
            pltpu.VMEM((EXC, RN, 4, ZN, 128), F32),
            pltpu.VMEM((EXC, RN, 4, ZN, 128), F32),
            pltpu.VMEM((EXC, RN + 2 * PAD, 4, ZN, 128), F32),
            pltpu.VMEM((EXC, RN, 4, ZN, 128), F32),
            pltpu.VMEM((EXC, ZN * ROWS, 128), F32),
            pltpu.VMEM((EXC, ZN * ROWS, 128), F32),
            pltpu.VMEM((4, 144, 128), F32),
            pltpu.VMEM((512, 128), F32),
            pltpu.VMEM((EXC, 16, 4096), F32),
            pltpu.VMEM((BASES, 32, 128), F32),
            pltpu.VMEM((2 * RN + 4 * PAD, 3, BASES, ZN, 128), F32),
            pltpu.VMEM((3, BASES, 144, 128), F32),
            pltpu.VMEM((4, 2, 3, 2, BASES, 8, 128), F32),
            pltpu.VMEM((4, 3, ZN, 128), F32),
            pltpu.VMEM((256, 128), BF16),
            pltpu.VMEM((256, 128), BF16),
            pltpu.VMEM((256, 128), BF16),
            pltpu.VMEM((256, 128), BF16),
            pltpu.VMEM((256, 512), F32),
            pltpu.VMEM((512, 256), BF16),
            pltpu.VMEM((512, 256), BF16),
            pltpu.VMEM((2, 288, 256), F32),
            pltpu.VMEM((2, 288, 128), F32),
            pltpu.VMEM((256, 512), F32),
            pltpu.VMEM((256, 256), F32),
            dma((10,)), dma((EXC,)), dma((EXC,)), dma(()), dma(()),
            dma((EXC,)), dma((EXC,)), dma((EXC,)), dma((EXC,)),
            dma((EXC,)), dma((EXC,)), dma((EXC,)),
        ],
        compiler_params=pltpu.CompilerParams(
            collective_id=0, has_side_effects=True, vmem_limit_bytes=50 * 2**20
        ),
        name="two_stage_adjoint",
    )(*(
        pltpu.with_memory_space_constraint(x, pltpu.HBM)
        for x in (
            top_adj,
            level1_adj.reshape(EXC, 512, 128),
            image_offsets.T,
            image_weights.reshape(1, 32),
            incidence.T,
            child_list.T,
            theta_index_top.T,
            theta_weight_top.T,
            phi_weight_top.T,
            theta_index_mid.T,
            theta_weight_mid.T,
            phi_weight_mid.T,
        )
    ))


def solution(mesh):
    placed = (
        P("rhs", "dev", None, None),
        P("rhs", "dev", None, None),
        P("rhs", None),
        P("rhs"),
        P(),
        P(),
        P(),
        P(),
        P(),
        P(),
        P(),
        P(),
    )
    return jax.shard_map(
        local, mesh=mesh, in_specs=placed, out_specs=P("rhs", "dev", None), check_vma=False
    )
```

```python
import math

import jax
import jax.numpy as jnp
from jax import lax
from jax.experimental import pallas as pl
from jax.experimental.pallas import tpu as pltpu
from jax.sharding import PartitionSpec as P

PHASE_TOP = 18.85
PHASE_MID = 9.42
LATTICE = 12.57

F32 = jnp.float32
BF16 = jnp.bfloat16

EXC = 8
RN = 16
ZN = 8
PAD = 2
BASES = 4
IMAGES = 64
AHEAD = 1
LAG = 2
ROWS = 72


FAR_FIRST = (
    (2, 2), (2, 3), (1, 2), (3, 3), (3, 2), (1, 3), (2, 0), (0, 2), (2, 1), (0, 3),
    (1, 0), (3, 1), (3, 0), (1, 1), (0, 1),
)


def iota(shape, dim):
    return lax.broadcasted_iota(jnp.int32, shape, dim)


def column(row):
    n = row.shape[1]
    square = jnp.where(iota((n, n), 0) == iota((n, n), 1), jnp.broadcast_to(row, (n, n)), 0.0)
    return jnp.sum(square, axis=1, keepdims=True)


def split(x):
    high = x.astype(BF16)
    return high, (x - high.astype(F32)).astype(BF16)


def dot3(x, w_high, w_low):
    high, low = split(x)
    out = jnp.dot(high, w_high, preferred_element_type=F32)
    out += jnp.dot(low, w_high, preferred_element_type=F32)
    out += jnp.dot(high, w_low, preferred_element_type=F32)
    return out


def sincos(x):
    turns = jnp.floor(x * (2.0 / math.pi) + 0.5)
    rest = ((x - turns * 1.5703125) - turns * 4.837512969970703e-4) - turns * 7.549789954891882e-8
    z = rest * rest
    sine = ((-1.9515295891e-4 * z + 8.3321608736e-3) * z - 1.6666654611e-1) * z * rest + rest
    cosine = (
        ((2.443315711809948e-5 * z - 1.388731625493765e-3) * z + 4.166664568298827e-2) * z * z
        - 0.5 * z + 1.0
    )
    quadrant = turns.astype(jnp.int32) & 3
    odd = (quadrant & 1) == 1
    out_sin = jnp.where(odd, cosine, sine)
    out_cos = jnp.where(odd, sine, cosine)
    out_sin = jnp.where(quadrant >= 2, -out_sin, out_sin)
    out_cos = jnp.where(((quadrant + 1) & 2) == 2, -out_cos, out_cos)
    return out_sin, out_cos


def bases(factor, theta, azimuth):
    sin_theta, _ = sincos(theta)
    sin_phi, cos_phi = sincos(azimuth)
    sin_x, cos_x = sincos(factor * (cos_phi * sin_theta))
    sin_y, cos_y = sincos(factor * (sin_phi * sin_theta))
    return cos_x * cos_y, sin_x * sin_y, sin_x * cos_y, cos_x * sin_y


def theta_rows(index_ref, weight_ref, columns):
    samples = index_ref.shape[1]
    rows = iota((columns, samples), 0)
    total = jnp.zeros((columns, samples), F32)
    for s in range(3):
        hit = rows == jnp.broadcast_to(index_ref[s : s + 1, :], (columns, samples))
        total += jnp.where(hit, jnp.broadcast_to(weight_ref[s : s + 1, :], (columns, samples)), 0.0)
    return total


def kernel(
    top_hbm, lvl_hbm, off_hbm, wgt_hbm, inc_hbm, child_hbm, tit_hbm, twt_hbm, pwt_hbm,
    tim_hbm, twm_hbm, pwm_hbm,
    out_hbm,
    off_ref, wgt_ref, inc_ref, child_ref, tit_ref, twt_ref, pwt_ref, tim_ref, twm_ref, pwm_ref,
    tin, lin, lat_own, lat_far, lattice,
    s1t, s1l, r1t, r1l, sb, r2, gq, ot, ov,
    btab, wtab, wb, wtab2, signs,
    wab_h, wab_l, wgd_h, wgd_l, w2t, w2_h, w2_l,
    xs, tq, x2, y2,
    sem_small, sem_tin, sem_lin, sem_img_s, sem_img_r,
    ss_t, rs_t, ss_l, rs_l, ss_2, rs_2, sem_out,
):
    dev = lax.axis_index("dev")
    rhs = lax.axis_index("rhs")
    z = dev // RN
    r = dev % RN

    barrier = pltpu.get_barrier_semaphore()

    def greet_plane(o, _):
        pl.semaphore_signal(
            barrier, inc=1, device_id={"dev": z * RN + (r + o) % RN},
            device_id_type=pl.DeviceIdType.MESH,
        )
        return 0

    def greet_column(o, _):
        pl.semaphore_signal(
            barrier, inc=1, device_id={"dev": (z + o) % ZN * RN + r},
            device_id_type=pl.DeviceIdType.MESH,
        )
        return 0

    lax.fori_loop(1, RN, greet_plane, 0)
    lax.fori_loop(1, ZN, greet_column, 0)
    pl.semaphore_signal(
        barrier, inc=1, device_id={"rhs": 1 - rhs}, device_id_type=pl.DeviceIdType.MESH
    )

    smalls = [
        pltpu.make_async_copy(source, target, sem_small.at[k])
        for k, (source, target) in enumerate((
            (off_hbm, off_ref), (wgt_hbm, wgt_ref), (inc_hbm, inc_ref), (child_hbm, child_ref),
            (tit_hbm, tit_ref), (twt_hbm, twt_ref), (pwt_hbm, pwt_ref), (tim_hbm, tim_ref),
            (twm_hbm, twm_ref), (pwm_hbm, pwm_ref),
        ))
    ]
    for copy in smalls[:3]:
        copy.start()

    def start_inputs(e, _):
        pltpu.make_async_copy(lvl_hbm.at[e], lin.at[e], sem_lin.at[e]).start()
        for p in range(2):
            for c in range(2):
                pltpu.make_async_copy(
                    top_hbm.at[e, p, :, pl.ds(c * 128, 128)], tin.at[e, p, c], sem_tin.at[e]
                ).start()
        return 0

    lax.fori_loop(0, EXC, start_inputs, 0)
    for copy in smalls[3:]:
        copy.start()

    def pack_level(e):
        pltpu.make_async_copy(lin.at[e], lin.at[e], sem_lin.at[e]).wait()

        def body(q, _):
            for j in range(4):
                s1l[e, q, j] = lin[e, pl.ds(4 * q + j, ZN, stride=4 * RN), :]
            return 0

        lax.fori_loop(0, RN, body, 0)

    def pack_top(e):
        pltpu.make_async_copy(tin.at[e], tin.at[e], sem_tin.at[e]).wait()
        factors = []
        for p in range(2):
            for c in range(2):
                factors.append(jnp.broadcast_to(lattice[p, c, pl.ds(e, 1), :], (ZN, 128)))

        def body(q, _):
            for p in range(2):
                s_re, s_im = factors[2 * p], factors[2 * p + 1]
                a_re = tin[e, p, 0, pl.ds(q, ZN, stride=RN), :]
                a_im = tin[e, p, 1, pl.ds(q, ZN, stride=RN), :]
                s1t[e, q, 2 * p] = s_re * a_re + s_im * a_im
                s1t[e, q, 2 * p + 1] = s_re * a_im - s_im * a_re
            return 0

        lax.fori_loop(0, RN, body, 0)

    def send_plane(e, source, target, send_sem, recv_sem, first):
        for over, across in FAR_FIRST:
            peer = (
                (r // 4 + over) % 4 * 4 + (r // 2 + across // 2) % 2 * 2 + (r + across) % 2
            )
            pltpu.make_async_remote_copy(
                src_ref=source.at[e, peer], dst_ref=target.at[e, first + r],
                send_sem=send_sem.at[e], recv_sem=recv_sem.at[e],
                device_id={"dev": z * RN + peer}, device_id_type=pl.DeviceIdType.MESH,
            ).start()
        pltpu.make_async_copy(source.at[e, r], target.at[e, first + r], recv_sem.at[e]).start()

    def wait_bytes(ref, sem):
        pltpu.make_async_copy(ref, ref, sem).wait()

    for copy in smalls[:3]:
        copy.wait()
    theta = (math.pi / 128) * (iota((8, 128), 1).astype(F32) + 0.5)
    own_phi = (2 * math.pi / 256) * (2 * dev + iota((8, 128), 0)).astype(F32)
    sin_theta, _ = sincos(theta)
    sin_phi, cos_phi = sincos(own_phi)
    own_x = cos_phi * sin_theta
    own_y = sin_phi * sin_theta
    off_x = column(off_ref[0:1, :].astype(F32))
    off_y = column(off_ref[1:2, :].astype(F32))
    weight = column(wgt_ref[...]) * (float(IMAGES) ** -0.5)
    turn = -LATTICE * (off_x * inc_ref[0:1, :] + off_y * inc_ref[1:2, :])
    coef_im, coef_re = (weight * value for value in sincos(turn))
    waves = []
    for p in range(2):
        angle = LATTICE * (off_x * own_x[p : p + 1, :] + off_y * own_y[p : p + 1, :])
        waves.extend(reversed(sincos(angle)))
    waves = jnp.concatenate(waves, axis=1)
    with_re, with_im = (
        lax.dot_general(
            coef, waves, (((0,), (0,)), ((), ())), precision=lax.Precision.HIGHEST,
            preferred_element_type=F32,
        )
        for coef in (coef_re, coef_im)
    )
    for p in range(2):
        at = 256 * p
        total = (
            with_re[:, at : at + 128] - with_im[:, at + 128 : at + 256],
            with_re[:, at + 128 : at + 256] + with_im[:, at : at + 128],
        )
        for c in range(2):
            for k in range(2):
                lat_own[k, p, c] = total[c][EXC * k : EXC * (k + 1), :]

    pack_level(0)
    pl.semaphore_wait(barrier, RN - 1 + ZN - 1 + 1)
    swap = pltpu.make_async_remote_copy(
        src_ref=lat_own.at[1 - rhs], dst_ref=lat_far, send_sem=sem_img_s, recv_sem=sem_img_r,
        device_id={"rhs": 1 - rhs}, device_id_type=pl.DeviceIdType.MESH,
    )
    swap.start()
    send_plane(0, s1l, r1l, ss_l, rs_l, 0)
    swap.wait()
    lattice[...] = lat_own[rhs] + lat_far[...]
    pack_top(0)
    send_plane(0, s1t, r1t, ss_t, rs_t, PAD)

    def send_both(e, _):
        pack_top(e)
        send_plane(e, s1t, r1t, ss_t, rs_t, PAD)
        pack_level(e)
        send_plane(e, s1l, r1l, ss_l, rs_l, 0)
        return 0

    lax.fori_loop(1, AHEAD, send_both, 0)

    zeros = jnp.zeros((ZN, 128), F32)

    def clear_top(e, _):
        for k in range(PAD):
            for c in range(4):
                r1t[e, k, c] = zeros
                r1t[e, PAD + RN + k, c] = zeros
        return 0

    lax.fori_loop(0, EXC, clear_top, 0)

    def clear_weights(k, _):
        for s in range(3):
            for b in range(BASES):
                wtab[k, s, b] = zeros
                wtab[2 * RN + 2 * PAD + k, s, b] = zeros
        return 0

    lax.fori_loop(0, 2 * PAD, clear_weights, 0)

    for copy in smalls[3:]:
        copy.wait()
    theta_b = (math.pi / 128) * (iota((32, 128), 1).astype(F32) + 0.5)
    phi_b = (2 * math.pi / 256) * (32 * z + iota((32, 128), 0)).astype(F32)
    for b, value in enumerate(bases(PHASE_TOP, theta_b, phi_b)):
        btab[b] = value
    mid_t = (iota((144, 128), 1) % 64).astype(F32)
    theta_b = (math.pi / 64) * (mid_t + 0.5)
    mid_p = (iota((144, 128), 0) + 120) % 128
    mid_bases = bases(PHASE_MID, theta_b, (2 * math.pi / 128) * mid_p.astype(F32))
    own_lane = mid_p == iota((144, 128), 1)
    for s in range(3):
        row = jnp.broadcast_to(pwm_ref[s : s + 1, :], (144, 128))
        weights = jnp.sum(jnp.where(own_lane, row, 0.0), axis=1, keepdims=True)
        for b in range(BASES):
            wb[s, b] = weights * mid_bases[b]

    def weigh_top(p, _):
        for b in range(BASES):
            row = jnp.broadcast_to(btab[b, pl.ds(p, 1), :], (ZN, 128))
            for s in range(3):
                wtab[2 * PAD + p, s, b] = row * pwt_ref[s, 32 * z + p]
        return 0

    lax.fori_loop(0, 2 * RN, weigh_top, 0)

    def weigh_mid(g, _):
        for odd in range(2):
            for s in range(3):
                for h in range(2):
                    first = 32 * g + 2 * (odd - s) + 10 + h
                    for b in range(BASES):
                        wtab2[g, odd, s, h, b] = wb[s, b, pl.ds(first, 8, stride=4), :]
        return 0

    lax.fori_loop(0, 4, weigh_mid, 0)

    own_box = iota((ZN, 128), 1) == RN * iota((ZN, 128), 0) + r
    own_first = (4 * (RN * iota((ZN, 1), 0) + r)).astype(F32)
    places = []
    for j in range(4):
        row = jnp.broadcast_to(child_ref[j : j + 1, :].astype(F32), (ZN, 128))
        places.append(jnp.sum(jnp.where(own_box, row, 0.0), axis=1, keepdims=True) - own_first)
    for i in range(4):
        sign_x = jnp.zeros((ZN, 1), F32)
        sign_y = jnp.zeros((ZN, 1), F32)
        for j in range(4):
            here = jnp.where(places[j] == float(i), 1.0, 0.0)
            sign_x += (2.0 * (j % 2) - 1.0) * here
            sign_y += (2.0 * (j // 2) - 1.0) * here
        signs[i, 0] = jnp.broadcast_to(sign_x * sign_y, (ZN, 128))
        signs[i, 1] = jnp.broadcast_to(sign_x, (ZN, 128))
        signs[i, 2] = jnp.broadcast_to(sign_y, (ZN, 128))

    theta_t = theta_rows(tit_ref, twt_ref, 64)
    along_z = PHASE_TOP * sincos((math.pi / 128) * (iota((1, 128), 1).astype(F32) + 0.5))[1]
    sin_z, cos_z = sincos(along_z)
    with_cos = theta_t * cos_z
    with_sin = theta_t * sin_z

    def square(upper_left, upper_right, lower_left, lower_right):
        upper = jnp.concatenate([upper_left, upper_right], axis=1)
        lower = jnp.concatenate([lower_left, lower_right], axis=1)
        return jnp.concatenate([upper, lower], axis=0)

    wab_h[...], wab_l[...] = split(square(with_cos, with_sin, -with_sin, with_cos).T)
    wgd_h[...], wgd_l[...] = split(square(with_sin, -with_cos, with_cos, with_sin).T)

    theta_m = theta_rows(tim_ref, twm_ref, 32)
    theta_m = jnp.concatenate([theta_m, theta_m], axis=1)
    lane = iota((1, 128), 1)
    along_z = PHASE_MID * sincos((math.pi / 64) * ((lane % 64).astype(F32) + 0.5))[1]
    sin_z, cos_z = sincos(along_z)
    low = lane < 64
    rows = (
        (jnp.where(low, cos_z, sin_z), jnp.where(low, -sin_z, cos_z)),
        (jnp.where(low, sin_z, -cos_z), jnp.where(low, cos_z, sin_z)),
    )
    for j in range(4):
        sign_x = 2.0 * (j % 2) - 1.0
        sign_y = 2.0 * (j // 2) - 1.0
        for c in range(2):
            for b, sign in enumerate((1.0, -sign_x * sign_y, sign_x, sign_y)):
                w2t[pl.ds(64 * j + 32 * c, 32), pl.ds(128 * b, 128)] = theta_m * (
                    sign * rows[b // 2][c]
                )
    w2_h[...], w2_l[...] = split(w2t[...].T)

    def upper(e):
        wait_bytes(r1t.at[e, pl.ds(PAD, RN)], rs_t.at[e])

        def stencil(q, _):
            total = [[None, None] for _ in range(BASES)]
            for s in range(3):
                for h in range(2):
                    slot = q - s + PAD
                    data = [r1t[e, slot, 2 * h + c] for c in range(2)]
                    for b in range(BASES):
                        factor = wtab[2 * slot + h, s, b]
                        for c in range(2):
                            term = factor * data[c]
                            total[b][c] = term if total[b][c] is None else total[b][c] + term
            for b in range(BASES):
                for c in range(2):
                    xs[b // 2, pl.ds(144 * (b % 2) + 8 * q, 8), pl.ds(128 * c, 128)] = total[b][c]
            return 0

        lax.fori_loop(0, RN + 2, stencil, 0, unroll=2)
        tq[0] = dot3(xs[0], wab_h[...], wab_l[...])
        tq[1] = dot3(xs[1], wgd_h[...], wgd_l[...])

        def combine(q):
            part = [tq[b // 2, pl.ds(144 * (b % 2) + 8 * q, 8), :] for b in range(BASES)]
            return [
                part[0] - signs[i, 0] * part[1] + signs[i, 1] * part[2] + signs[i, 2] * part[3]
                for i in range(4)
            ]

        def inner(q, _):
            for i, value in enumerate(combine(q + 1)):
                sb[e, pl.ds(16 * i + q, ZN, stride=ROWS), :] = r1l[e, q, i] + value
            return 0

        wait_bytes(r1l.at[e], rs_l.at[e])
        lax.fori_loop(0, RN, inner, 0, unroll=2)
        for side, q in enumerate((0, RN + 1)):
            for i, value in enumerate(combine(q)):
                sb[e, pl.ds(64 + 2 * i + side, ZN, stride=ROWS), :] = value

        for o in (4, 3, 5, 2, 6, 1, 7):
            peer = (z + o) % ZN
            pltpu.make_async_remote_copy(
                src_ref=sb.at[e, pl.ds(ROWS * peer, ROWS), :],
                dst_ref=r2.at[e, pl.ds(ROWS * z, ROWS), :],
                send_sem=ss_2.at[e], recv_sem=rs_2.at[e],
                device_id={"dev": peer * RN + r}, device_id_type=pl.DeviceIdType.MESH,
            ).start()
        pltpu.make_async_copy(
            sb.at[e, pl.ds(ROWS * z, ROWS), :], r2.at[e, pl.ds(ROWS * z, ROWS), :], rs_2.at[e]
        ).start()

    half = iota((8, 128), 1) < 64

    def lower(e):
        wait_bytes(r2.at[e], rs_2.at[e])

        def gather(k, _):
            for i in range(4):
                gq[i, pl.ds(8 + 16 * k, 16), :] = r2[e, pl.ds(ROWS * k + 16 * i, 16), :]
            return 0

        lax.fori_loop(0, ZN, gather, 0)
        for i in range(4):
            gq[i, pl.ds(0, 8), :] = zeros
            gq[i, pl.ds(136, 8), :] = zeros
            for side in range(2):
                halo = r2[e, pl.ds(64 + 2 * i + side, ZN, stride=ROWS), :]
                gq[i, pl.ds(7 + 17 * side, ZN, stride=16), :] += halo
            gq[i, pl.ds(135, 1), :] += gq[i, pl.ds(7, 1), :]
            gq[i, pl.ds(8, 1), :] += gq[i, pl.ds(136, 1), :]
            gq[i, pl.ds(6, 2), :] = gq[i, pl.ds(134, 2), :]
            gq[i, pl.ds(136, 2), :] = gq[i, pl.ds(8, 2), :]

        def stencil(g, _):
            for i in range(4):
                data = {
                    (shift, h): gq[i, pl.ds(32 * g + 2 * shift + 10 + h, 8, stride=4), :]
                    for shift in range(-2, 2)
                    for h in range(2)
                }
                for odd in range(2):
                    for b in range(BASES):
                        total = None
                        for s in range(3):
                            for h in range(2):
                                term = wtab2[g, odd, s, h, b] * data[odd - s, h]
                                total = term if total is None else total + term
                        x2[pl.ds(128 * odd + 32 * i + 8 * g, 8), pl.ds(128 * b, 128)] = total
            return 0

        lax.fori_loop(0, 4, stencil, 0, unroll=2)
        y2[...] = dot3(x2[...], w2_h[...], w2_l[...])

        def place(g, _):
            for i in range(4):
                for k in range(2):
                    a = y2[pl.ds(32 * i + 8 * g, 8), pl.ds(128 * k, 128)]
                    b = y2[pl.ds(128 + 32 * i + 8 * g, 8), pl.ds(128 * k, 128)]
                    row = 256 * (i // 2) + 64 * g + 4 * (i % 2) + 2 * k
                    ot[pl.ds(row, 8, stride=8), :] = jnp.where(half, a, pltpu.roll(b, 64, 1))
                    ot[pl.ds(row + 1, 8, stride=8), :] = jnp.where(half, pltpu.roll(a, 64, 1), b)
            return 0

        lax.fori_loop(0, 4, place, 0, unroll=2)
        for k in range(2):
            for m in range(32):
                ov[e, pl.ds(8 * k, 8), pl.ds(128 * m, 128)] = ot[pl.ds(256 * k + 8 * m, 8), :]
        pltpu.make_async_copy(ov.at[e], out_hbm.at[e], sem_out.at[e]).start()

    def levels(e, _):
        @pl.when(e < EXC - AHEAD)
        def _():
            send_both(e + AHEAD, 0)

        @pl.when(e < EXC)
        def _():
            upper(e)

        @pl.when(e >= LAG)
        def _():
            lower(e - LAG)

        return 0

    lax.fori_loop(0, EXC + LAG, levels, 0)

    def drain(e, _):
        wait_bytes(s1l.at[e, pl.ds(0, RN - 1)], ss_l.at[e])
        wait_bytes(s1t.at[e, pl.ds(0, RN - 1)], ss_t.at[e])
        wait_bytes(sb.at[e, pl.ds(0, ROWS * (ZN - 1))], ss_2.at[e])
        pltpu.make_async_copy(ov.at[e], out_hbm.at[e], sem_out.at[e]).wait()
        return 0

    lax.fori_loop(0, EXC, drain, 0)


def local(
    top_adj,
    level1_adj,
    image_offsets,
    image_weights,
    incidence,
    child_list,
    theta_index_top,
    theta_weight_top,
    phi_weight_top,
    theta_index_mid,
    theta_weight_mid,
    phi_weight_mid,
):
    anywhere = pl.BlockSpec(memory_space=pl.ANY)
    hbm = pl.BlockSpec(memory_space=pltpu.HBM)
    dma = pltpu.SemaphoreType.DMA
    return pl.pallas_call(
        kernel,
        out_shape=jax.ShapeDtypeStruct((EXC, 16, 4096), F32),
        in_specs=[hbm] * 12,
        out_specs=anywhere,
        scratch_shapes=[
            pltpu.VMEM((2, 32), jnp.int32),
            pltpu.VMEM((1, 32), F32),
            pltpu.VMEM((2, 16), F32),
            pltpu.VMEM((4, 128), jnp.int32),
            pltpu.VMEM((3, 128), jnp.int32),
            pltpu.VMEM((3, 128), F32),
            pltpu.SMEM((3, 256), F32),
            pltpu.VMEM((3, 64), jnp.int32),
            pltpu.VMEM((3, 64), F32),
            pltpu.VMEM((3, 128), F32),
            pltpu.VMEM((EXC, 2, 2, 128, 128), F32),
            pltpu.VMEM((EXC, 512, 128), F32),
            pltpu.VMEM((2, 2, 2, EXC, 128), F32),
            pltpu.VMEM((2, 2, EXC, 128), F32),
            pltpu.VMEM((2, 2, EXC, 128), F32),
            pltpu.VMEM((EXC, RN, 4, ZN, 128), F32),
            pltpu.VMEM((EXC, RN, 4, ZN, 128), F32),
            pltpu.VMEM((EXC, RN + 2 * PAD, 4, ZN, 128), F32),
            pltpu.VMEM((EXC, RN, 4, ZN, 128), F32),
            pltpu.VMEM((EXC, ZN * ROWS, 128), F32),
            pltpu.VMEM((EXC, ZN * ROWS, 128), F32),
            pltpu.VMEM((4, 144, 128), F32),
            pltpu.VMEM((512, 128), F32),
            pltpu.VMEM((EXC, 16, 4096), F32),
            pltpu.VMEM((BASES, 32, 128), F32),
            pltpu.VMEM((2 * RN + 4 * PAD, 3, BASES, ZN, 128), F32),
            pltpu.VMEM((3, BASES, 144, 128), F32),
            pltpu.VMEM((4, 2, 3, 2, BASES, 8, 128), F32),
            pltpu.VMEM((4, 3, ZN, 128), F32),
            pltpu.VMEM((256, 128), BF16),
            pltpu.VMEM((256, 128), BF16),
            pltpu.VMEM((256, 128), BF16),
            pltpu.VMEM((256, 128), BF16),
            pltpu.VMEM((256, 512), F32),
            pltpu.VMEM((512, 256), BF16),
            pltpu.VMEM((512, 256), BF16),
            pltpu.VMEM((2, 288, 256), F32),
            pltpu.VMEM((2, 288, 128), F32),
            pltpu.VMEM((256, 512), F32),
            pltpu.VMEM((256, 256), F32),
            dma((10,)), dma((EXC,)), dma((EXC,)), dma(()), dma(()),
            dma((EXC,)), dma((EXC,)), dma((EXC,)), dma((EXC,)),
            dma((EXC,)), dma((EXC,)), dma((EXC,)),
        ],
        compiler_params=pltpu.CompilerParams(
            collective_id=0, has_side_effects=True, vmem_limit_bytes=50 * 2**20
        ),
        name="two_stage_adjoint",
    )(*(
        pltpu.with_memory_space_constraint(x, pltpu.HBM)
        for x in (
            top_adj,
            level1_adj.reshape(EXC, 512, 128),
            image_offsets.T,
            image_weights.reshape(1, 32),
            incidence.T,
            child_list.T,
            theta_index_top.T,
            theta_weight_top.T,
            phi_weight_top.T,
            theta_index_mid.T,
            theta_weight_mid.T,
            phi_weight_mid.T,
        )
    ))


def solution(mesh):
    placed = (
        P("rhs", "dev", None, None),
        P("rhs", "dev", None, None),
        P("rhs", None),
        P("rhs"),
        P(),
        P(),
        P(),
        P(),
        P(),
        P(),
        P(),
        P(),
    )
    return jax.shard_map(
        local, mesh=mesh, in_specs=placed, out_specs=P("rhs", "dev", None), check_vma=False
    )
```
